512 devices in a mesh: voxel: 32 (over x, z_lo, core), feature: 4 (over z_hi), tm: 4 (over y).
Axes of the slice: x: 4, y: 4, z: 16 (z_hi: 4, z_lo: 4; z = z_hi * 4 + z_lo), core: 2. Of those that a mesh axis runs over, the one named last changes fastest.
Arguments:
- hidden: bfloat16 [3072, 8192], P('tm', 'feature'), may hold values from -6 to 6
- bold: bfloat16 [3072, 4096], P('tm', 'voxel'), may hold values from -6 to 6
- panel: bfloat16 [65536, 128], P(('feature', 'tm'), 'voxel'), may hold values from -0.0234375 to 0.0234375
- eigvals: float32 [128], replicated, may hold values from 0.05 to 2
- ridge_grid: int32 [24], replicated, may hold values from 0 to 16
- delays: int32 [8], replicated, may hold values from 1 to 12, as said below
- runs: int32 [3072], replicated, may hold values from 0 to 7, never falling along the last dimension, each value on 1 to 768 neighbouring positions
Outputs:
- scaled: bfloat16 [24, 128, 4096], P(None, None, 'voxel')
The draws below stay inside these ranges and needn't reach their ends.
Inputs may be any that keep to these rules, and one draw needn't show every extreme that they name: 8 distinct delays, 12 among them. `runs`: run numbers never fall along the TRs; a run holds 1 to 768 TRs.
All inputs are finite; a program needn't handle non-finite values.
Results may differ from the reference program's by a relative error of at most 0.022.
Values may be sent and summed in bfloat16 or wider, within the bound.
A program may use at most 64 MiB of HBM per device.

```python
import math
import jax
import jax.numpy as jnp
import numpy as np
from jax import lax

D = 8192
DELAYS = 8
MAXD = 12
T_DEV = 768
V_DEV = 128
PANEL = 128
RIDGES = 24
FEATS = 65536
TRS = 3072
VOX = 4096
N_TM = 4


def draw_delays(key, part):
    others = jax.random.permutation(key, MAXD - 1) + 1
    picked = jnp.concatenate([jnp.full((1,), MAXD, jnp.int32), others[:DELAYS - 1].astype(jnp.int32)])
    return jax.random.permutation(jax.random.fold_in(key, 7), picked).astype(jnp.int32)


def place_ends(entries, key, low, top_value):
    place = [jax.random.randint(jax.random.fold_in(key, axis), (), 0, length) for axis, length in enumerate(entries.shape)]
    main_axis = entries.shape.index(max(entries.shape))
    neighbour = place[:main_axis] + [(place[main_axis] + 1) % entries.shape[main_axis]] + place[main_axis + 1:]
    return entries.at[tuple(place)].set(low).at[tuple(neighbour)].set(top_value)


def block_scale(rng, dims, split, least, high):
    loudness = 1.0
    for dim, shards_of in split:
        draws = jax.random.uniform(jax.random.fold_in(jax.random.fold_in(rng, 6), dim), (shards_of,), jnp.float32, least / len(split), high / len(split))
        loudness = loudness * jnp.repeat(jnp.exp(draws), dims[dim] // shards_of).reshape((-1,) + (1,) * (len(dims) - 1 - dim))
    return loudness


def split_up(number_of, total, bound, slope):
    weights = [(1 << 20) // math.isqrt(rank ** slope) + 1 for rank in range(2, number_of + 1)]
    surplus, holding = total - bound - (number_of - 1), [1] * (number_of - 1)
    while surplus > 0:
        candidates = [i for i in range(number_of - 1) if holding[i] < bound]
        whole, remaining = sum([weights[i] for i in candidates]), surplus
        for i in candidates:
            extra = min(bound - holding[i], max(1, remaining * weights[i] // whole), surplus)
            holding[i] = holding[i] + extra
            surplus = surplus - extra
    return np.array([bound] + holding)


def ragged(key, amount, total, limit, skew):
    if amount == 2:
        one = jax.random.randint(key, (), max(1, total - limit), min(limit, total - 1) + 1)
        return jnp.stack([one, total - one])
    lengths = jnp.asarray(split_up(amount, total, limit, skew), jnp.int32)
    twos = (amount - 1) // 2
    source_of, receiver = lengths[1:1 + 2 * twos:2], lengths[2:2 + 2 * twos:2]
    slack = jnp.minimum(source_of - 1, limit - receiver)
    shifted = jax.random.randint(jax.random.fold_in(key, 1), (twos,), 0, 1 << 20) % (slack + 1)
    lengths = lengths.at[1:1 + 2 * twos:2].set(source_of - shifted).at[2:2 + 2 * twos:2].set(receiver + shifted)
    return lengths[jax.random.permutation(jax.random.fold_in(key, 2), amount)]


def normal_values(rng, extent, deviation, limit, shards=(), held_as=jnp.bfloat16):
    loudness = block_scale(rng, extent, shards, -0.22, 0.18) if shards else 1.0
    entries = jax.random.normal(rng, extent, jnp.float32) * deviation * loudness
    return jnp.minimum(jnp.maximum(entries, -limit), limit).astype(held_as)


def setup_inputs(seed: int = 0) -> dict:
    keys = jax.random.split(jax.random.key(seed), 8)
    return {
        "hidden": normal_values(keys[0], (TRS, D), 1.0, 6.0, ((0, 4), (1, 4))),
        "bold": normal_values(keys[1], (TRS, VOX), 1.0, 6.0, ((0, 4), (1, 32))),
        "panel": normal_values(keys[2], (FEATS, PANEL), FEATS ** -0.5, 0.0234375, ((0, 16), (1, 32))),
        "eigvals": jnp.clip(jnp.exp(jax.random.uniform(keys[3], (PANEL,), jnp.float32, math.log(0.05), math.log(2.0))), 0.05, 2.0),
        "ridge_grid": place_ends(jax.random.randint(keys[4], (RIDGES,), 0, 17), jax.random.fold_in(keys[4], 1), 0, 16).astype(jnp.int32),
        "delays": draw_delays(jax.random.fold_in(keys[7], 71), 0),
        "runs": jnp.searchsorted(jnp.cumsum(ragged(keys[6], 2 * N_TM, TRS, T_DEV, 2)), jnp.arange(TRS), side="right").astype(jnp.int32),
    }


def reference(hidden, bold, panel, eigvals, ridge_grid, delays, runs):
    steps_idx = jnp.arange(TRS, dtype=jnp.int32)
    runs_pad = jnp.concatenate([runs, jnp.full((MAXD,), -1, jnp.int32)])
    bold_pad = jnp.concatenate([bold, jnp.zeros((MAXD, VOX), jnp.bfloat16)], 0)
    lagged_list = []
    for slot in range(DELAYS):
        target = steps_idx + delays[slot]
        valid = (target < TRS) & (runs_pad[target] == runs)
        moved = bold_pad[target]
        lagged_list.append(jnp.where(valid[:, None], moved, jnp.zeros_like(moved)))
    lagged = jnp.stack(lagged_list, 1)
    basis = panel.astype(jnp.float32)
    blocks = VOX // V_DEV

    def one_block(index):
        start = (index * V_DEV).astype(jnp.int32)
        piece = lax.dynamic_slice_in_dim(lagged, start, V_DEV, 2)
        total = jnp.zeros((PANEL, V_DEV), jnp.float32)
        for shard in range(N_TM):
            rows_x = hidden[shard * T_DEV:(shard + 1) * T_DEV].astype(jnp.float32)
            rows_y = piece[shard * T_DEV:(shard + 1) * T_DEV].reshape(T_DEV, DELAYS * V_DEV).astype(jnp.float32)
            cross = jnp.dot(rows_x.T, rows_y, precision=lax.Precision.HIGHEST)
            partial_value = cross.reshape(D * DELAYS, V_DEV).astype(jnp.bfloat16).astype(jnp.float32)
            total = total + jnp.dot(basis.T, partial_value, precision=lax.Precision.HIGHEST)
        return total
    stacked = lax.map(one_block, jnp.arange(blocks, dtype=jnp.int32))
    rotated = jnp.transpose(stacked, (1, 0, 2)).reshape(PANEL, VOX)
    penalty = 2.0 ** ((ridge_grid.astype(jnp.float32) - 8.0) * 0.5)
    scaled = rotated[None] / (math.sqrt(TRS) * (eigvals[None, :, None] + penalty[:, None, None]))
    return scaled.astype(jnp.bfloat16)
```

```python
import functools
import math

import jax
import jax.numpy as jnp
from jax import lax
from jax.experimental import pallas as pl
from jax.experimental.pallas import tpu as pltpu
from jax.sharding import PartitionSpec as P

DELAYS = 8
MAXD = 12
LANES = 128
BF16 = jnp.bfloat16
F32 = jnp.float32


def iota(shape, dim):
    return lax.broadcasted_iota(jnp.int32, shape, dim)


def dot(left, right, dims=((1,), (0,))):
    return lax.dot_general(left, right, (dims, ((), ())), preferred_element_type=F32)


def kernel(
    sizes,
    delays_ref, ridge_ref, hidden_ref, bold_ref, panel_ref, eig_ref, runs_ref,
    out_ref,
    hid, bext, wbuf, pbuf, abuf, xbuf, rbuf, fbuf, masks,
    hid_sem, bold_sem, halo_sem, w_sem, a_sem, x_sem, r_sem, f_sem,
):
    n_v, n_f, n_t, t_rows, d_local, p_local = sizes
    d_chunk = d_local // n_t
    ext = t_rows + LANES
    n_c = ext // LANES
    i = lax.axis_index("voxel")
    f = lax.axis_index("feature")
    j = lax.axis_index("tm")

    hid_copies = [
        pltpu.make_async_copy(
            hidden_ref.at[:, pl.ds(c * d_chunk, d_chunk)], hid.at[c], hid_sem.at[c]
        )
        for c in range(n_t)
    ]
    bold_copy = pltpu.make_async_copy(bold_ref, bext.at[pl.ds(0, t_rows)], bold_sem)
    for copy in hid_copies:
        copy.start()
    bold_copy.start()
    bext[pl.ds(t_rows, LANES), :] = jnp.zeros((LANES, bext.shape[1]), BF16)

    def others(count, me, use):
        def body(step, carry):
            use(step, lax.rem(me + step, count))
            return carry
        lax.fori_loop(1, count, body, 0)

    barrier = pltpu.get_barrier_semaphore()

    def greet(axis):
        def use(step, peer):
            pl.semaphore_signal(
                barrier, inc=1, device_id={axis: peer}, device_id_type=pl.DeviceIdType.MESH
            )
        return use

    others(n_t, j, greet("tm"))
    others(n_f, f, greet("feature"))
    others(n_v, i, greet("voxel"))

    rows_local = panel_ref.shape[1]
    n_rows = DELAYS * p_local
    spread = (iota((n_rows, p_local), 0) % p_local == iota((n_rows, p_local), 1)).astype(BF16)
    tall = dot(spread, panel_ref[...])
    keep = iota(tall.shape, 1) % DELAYS == iota(tall.shape, 0) // p_local
    tall = jnp.where(keep, tall, 0.0).astype(BF16)
    block = DELAYS * LANES
    squeeze = (iota((block, LANES), 0) // DELAYS == iota((block, LANES), 1)).astype(BF16)
    for b in range(rows_local // block):
        part = dot(tall[:, b * block:(b + 1) * block], squeeze)
        wbuf[j, :, pl.ds(b * LANES, LANES)] = part.astype(BF16)

    pl.semaphore_wait(barrier, n_t + n_f + n_v - 3)

    def send(src, dst, sems, slot, axis, peer):
        return pltpu.make_async_remote_copy(
            src_ref=src, dst_ref=dst, send_sem=sems.at[0, slot], recv_sem=sems.at[1, slot],
            device_id={axis: peer}, device_id_type=pl.DeviceIdType.MESH,
        )

    before = lax.rem(j + n_t - 1, n_t)
    halo = pltpu.make_async_remote_copy(
        src_ref=bold_ref.at[pl.ds(0, 16)], dst_ref=bext.at[pl.ds(t_rows, 16)],
        send_sem=halo_sem.at[0], recv_sem=halo_sem.at[1],
        device_id={"tm": before}, device_id_type=pl.DeviceIdType.MESH,
    )
    w_sends = [
        send(wbuf.at[j], wbuf.at[j], w_sem, s - 1, "tm", lax.rem(j + s, n_t)) for s in range(1, n_t)
    ]
    for copy in w_sends:
        copy.start()
    halo.start()

    own_runs = runs_ref[:, pl.ds(pl.multiple_of(j * t_rows, LANES), t_rows)]
    next_runs = runs_ref[:, pl.ds(pl.multiple_of(lax.rem(j + 1, n_t) * t_rows, LANES), LANES)]
    runs = jnp.broadcast_to(jnp.concatenate([own_runs, next_runs], 1), (8, ext))
    end = jnp.where(j == n_t - 1, t_rows, ext)
    inside = iota((8, ext), 1) < end
    for m in range(1, MAXD + 1):
        same = (pltpu.roll(runs, m, 1) == runs) & inside
        masks[m - 1] = jnp.where(same, 1.0, 0.0)
    shape = (8 * MAXD, n_rows)
    lag = iota(shape, 0) // 8 + 1
    delay_of = iota(shape, 1) // p_local
    right_p = iota(shape, 0) % 8 == iota(shape, 1) % p_local
    wanted = jnp.zeros(shape, jnp.int32)
    for k in range(DELAYS):
        wanted = jnp.where(delay_of == k, delays_ref[k], wanted)
    pick = jnp.where(right_p & (wanted == lag), 1.0, 0.0).astype(BF16)
    pick = jnp.concatenate([pick, pick], 1)
    n_x = n_v * 8
    order = (
        (iota((n_x, n_x), 0) % n_v == iota((n_x, n_x), 1) // 8)
        & (iota((n_x, n_x), 0) // n_v == iota((n_x, n_x), 1) % 8)
    ).astype(BF16)

    for copy in hid_copies:
        copy.wait()
    nt = ((1,), (1,))
    g = dot(wbuf[j], hid[j], nt)
    for s in range(1, n_t):
        w_sends[s - 1].wait_recv()
        source = lax.rem(j + n_t - s, n_t)
        g = g + dot(wbuf[source], hid[source], nt)

    high = g.astype(BF16)
    low = (g - high.astype(F32)).astype(BF16)
    lagged = dot(pick, jnp.concatenate([high, low], 0))
    lagged = jnp.concatenate([lagged, jnp.zeros((8 * MAXD, LANES), F32)], 1)
    gs = jnp.zeros((8, ext), F32)
    for m in range(1, MAXD + 1):
        gs = gs + pltpu.roll(lagged[8 * (m - 1):8 * m], m, 1) * masks[m - 1]

    row = iota((8, LANES), 0)
    for p in range(p_local):
        tile = jnp.zeros((8, LANES), F32)
        for c in range(n_c):
            line = jnp.broadcast_to(gs[p:p + 1, c * LANES:(c + 1) * LANES], (8, LANES))
            tile = jnp.where(row == c, line, tile)
        pbuf[p] = tile.astype(BF16)
    abuf[f] = pbuf[f]
    a_sends = [
        send(pbuf.at[lax.rem(f + s, n_f)], abuf.at[f], a_sem, s - 1, "feature", lax.rem(f + s, n_f))
        for s in range(1, n_f)
    ]
    for copy in a_sends:
        copy.start()
    for copy in a_sends:
        copy.wait_recv()
    total = abuf[0].astype(F32)
    for s in range(1, n_f):
        total = total + abuf[s].astype(F32)
    xbuf[i] = total.astype(BF16)

    def x_send(step, peer):
        pltpu.make_async_remote_copy(
            src_ref=xbuf.at[i], dst_ref=xbuf.at[i], send_sem=x_sem.at[0], recv_sem=x_sem.at[1],
            device_id={"voxel": peer}, device_id_type=pl.DeviceIdType.MESH,
        ).start()

    others(n_v, i, x_send)
    halo.wait_recv()
    bold_copy.wait()
    arrived = xbuf.at[pl.ds(0, n_v - 1)]
    pltpu.make_async_copy(arrived, arrived, x_sem.at[1]).wait()

    x = dot(order, xbuf[...].reshape(n_x, LANES)).astype(BF16)
    r = jnp.zeros((n_v, bext.shape[1]), F32)
    for c in range(n_c):
        r = r + dot(x[c * n_v:(c + 1) * n_v], bext[pl.ds(c * LANES, LANES), :])
    rbuf[j] = r.astype(BF16)
    r_sends = [
        send(rbuf.at[j], rbuf.at[j], r_sem, s - 1, "tm", lax.rem(j + s, n_t)) for s in range(1, n_t)
    ]
    for copy in r_sends:
        copy.start()
    for copy in r_sends:
        copy.wait_recv()
    r = rbuf[0].astype(F32)
    for s in range(1, n_t):
        r = r + rbuf[s].astype(F32)

    fbuf[f] = r.astype(BF16)
    f_sends = [
        send(fbuf.at[f], fbuf.at[f], f_sem, s - 1, "feature", lax.rem(f + s, n_f))
        for s in range(1, n_f)
    ]
    for copy in f_sends:
        copy.start()
    for copy in f_sends:
        copy.wait_recv()
    for s in range(n_f):
        out_ref[pl.ds(s, n_v, stride=n_f), :] = fbuf[s].astype(F32)

    for copy in w_sends + a_sends + r_sends + f_sends + [halo]:
        copy.wait_send()
    pltpu.make_async_copy(arrived, arrived, x_sem.at[0]).wait()


def shards(hidden, bold, panel, eigvals, ridge_grid, delays, runs):
    n_v, n_f, n_t = (lax.axis_size(axis) for axis in ("voxel", "feature", "tm"))
    t_rows, d_local = hidden.shape
    v_cols = bold.shape[1]
    p_local = panel.shape[1]
    n_p = n_v * p_local
    assert p_local == n_f and n_v * 8 % 16 == 0
    ext = t_rows + LANES
    d_chunk = d_local // n_t
    vmem = pl.BlockSpec(memory_space=pltpu.VMEM)
    smem = pl.BlockSpec(memory_space=pltpu.SMEM)
    hbm = pl.BlockSpec(memory_space=pl.ANY)
    dma = pltpu.SemaphoreType.DMA
    rotated = pl.pallas_call(
        functools.partial(kernel, (n_v, n_f, n_t, t_rows, d_local, p_local)),
        out_shape=jax.ShapeDtypeStruct((n_p, v_cols), F32),
        in_specs=[smem, smem, hbm, hbm, vmem, vmem, vmem],
        out_specs=vmem,
        scratch_shapes=[
            pltpu.VMEM((n_t, t_rows, d_chunk), BF16),
            pltpu.VMEM((ext, v_cols), BF16),
            pltpu.VMEM((n_t, DELAYS * p_local, d_chunk), BF16),
            pltpu.VMEM((p_local, 8, LANES), BF16),
            pltpu.VMEM((n_f, 8, LANES), BF16),
            pltpu.VMEM((n_v, 8, LANES), BF16),
            pltpu.VMEM((n_t, n_v, v_cols), BF16),
            pltpu.VMEM((n_f, n_v, v_cols), BF16),
            pltpu.VMEM((MAXD, 8, ext), F32),
            dma((n_t,)),
            dma,
            dma((2,)),
            dma((2, n_t - 1)),
            dma((2, n_f - 1)),
            dma((2,)),
            dma((2, n_t - 1)),
            dma((2, n_f - 1)),
        ],
        compiler_params=pltpu.CompilerParams(collective_id=0, has_side_effects=True),
        name="sweep",
    )(delays, ridge_grid, hidden, bold, panel.T, eigvals[None], runs[None])
    penalty = 2.0 ** ((ridge_grid.astype(F32) - 8.0) * 0.5)
    scaled = rotated[None] / (
        math.sqrt(t_rows * n_t) * (eigvals[None, :, None] + penalty[:, None, None])
    )
    return scaled.astype(BF16)


def solution(mesh):
    return jax.shard_map(
        shards,
        mesh=mesh,
        in_specs=(
            P("tm", "feature"),
            P("tm", "voxel"),
            P(("feature", "tm"), "voxel"),
            P(),
            P(),
            P(),
            P(),
        ),
        out_specs=P(None, None, "voxel"),
        check_vma=False,
    )
```

```python
import functools
import math

import jax
import jax.numpy as jnp
from jax import lax
from jax.experimental import pallas as pl
from jax.experimental.pallas import tpu as pltpu
from jax.sharding import PartitionSpec as P

DELAYS = 8
MAXD = 12
LANES = 128
HALF = 512
N_ZLO = 4
BF16 = jnp.bfloat16
F32 = jnp.float32
MESH = pl.DeviceIdType.MESH


def iota(shape, dim):
    return lax.broadcasted_iota(jnp.int32, shape, dim)


def dot(left, right, dims=((1,), (0,))):
    return lax.dot_general(left, right, (dims, ((), ())), preferred_element_type=F32)


def kernel(
    sizes,
    delays_hbm, hidden_ref, bold_ref, panel_hbm, runs_hbm,
    out_ref,
    delays_ref, panel_ref, runs_ref,
    hid, bext, wbuf, abuf, xbuf, sbuf, rbuf, masks,
    in_sem, hid_sem, bold_sem, halo_sem, w_sem, a_sem, x_sem, r_sem, near_sem, far_sem,
):
    n_v, n_f, n_t, t_rows, d_local, p_local = sizes
    d_chunk = d_local // n_t
    ext = t_rows + LANES
    n_z = n_f * N_ZLO
    n_x = n_v // (2 * N_ZLO)
    i = lax.axis_index("voxel")
    f = lax.axis_index("feature")
    j = lax.axis_index("tm")
    core = lax.rem(i, 2)
    x = i // (2 * N_ZLO)
    z = f * N_ZLO + lax.rem(i // 2, N_ZLO)
    chip = i // 2

    def at(dx=0, dz=0, dj=0, flip=False):
        xx = lax.rem(x + dx, n_x)
        zz = lax.rem(z + dz + n_z, n_z)
        cc = 1 - core if flip else core
        return {
            "voxel": (xx * N_ZLO + lax.rem(zz, N_ZLO)) * 2 + cc,
            "feature": zz // N_ZLO,
            "tm": lax.rem(j + dj, n_t),
        }

    def signal(sem, where):
        pl.semaphore_signal(sem, inc=1, device_id=where, device_id_type=MESH)

    barrier = pltpu.get_barrier_semaphore()
    near = [at(dj=s, flip=w) for s in range(n_t) for w in (False, True) if s or w]
    near += [at(dx=s) for s in range(1, n_x)]
    along = [at(dz=s) for s in (-2, -1, 1, 2)]
    for where in near + along:
        signal(barrier, where)

    panel_copy = pltpu.make_async_copy(panel_hbm, panel_ref, in_sem.at[0])
    runs_copy = pltpu.make_async_copy(runs_hbm, runs_ref, in_sem.at[1])
    delays_copy = pltpu.make_async_copy(delays_hbm, delays_ref, in_sem.at[2])
    panel_copy.start()
    runs_copy.start()
    delays_copy.start()
    hid_copies = [
        pltpu.make_async_copy(
            hidden_ref.at[:, pl.ds(c * d_chunk, d_chunk)], hid.at[c], hid_sem.at[c]
        )
        for c in range(n_t)
    ]
    for copy in hid_copies:
        copy.start()
    bold_copy = pltpu.make_async_copy(bold_ref, bext.at[core, pl.ds(0, t_rows)], bold_sem.at[0])
    bold_copy.start()

    rows_local = panel_ref.shape[1]
    n_rows = DELAYS * p_local
    block = DELAYS * LANES
    spread = (iota((n_rows, p_local), 0) % p_local == iota((n_rows, p_local), 1)).astype(BF16)
    squeeze = (iota((block, LANES), 0) // DELAYS == iota((block, LANES), 1)).astype(BF16)
    keep = iota((n_rows, rows_local), 1) % DELAYS == iota((n_rows, rows_local), 0) // p_local
    panel_copy.wait()
    tall = dot(spread, panel_ref[...])
    tall = jnp.where(keep, tall, 0.0).astype(BF16)
    for b in range(rows_local // block):
        part = dot(tall[:, b * block:(b + 1) * block], squeeze)
        wbuf[j, :, pl.ds(b * LANES, LANES)] = part.astype(BF16)

    pl.semaphore_wait(barrier, len(near) + len(along))

    def remote(src, dst, sems, slot, where):
        return pltpu.make_async_remote_copy(
            src_ref=src, dst_ref=dst, send_sem=sems.at[0, slot], recv_sem=sems.at[1, slot],
            device_id=where, device_id_type=MESH,
        )

    w_sends = [remote(wbuf.at[j], wbuf.at[j], w_sem, s - 1, at(dj=s)) for s in range(1, n_t)]
    for copy in w_sends:
        copy.start()
    for where in along:
        signal(near_sem, where)
    tail = HALF * 2 - t_rows - 16
    for c in range(2):
        bext[c, pl.ds(t_rows + 16, tail), :] = jnp.zeros((tail, LANES), BF16)
    halos = [
        remote(
            bold_ref.at[pl.ds(0, 16)], bext.at[core, pl.ds(t_rows, 16)],
            halo_sem, s, at(dj=n_t - 1, flip=s == 1),
        )
        for s in range(2)
    ]
    share = pltpu.make_async_remote_copy(
        src_ref=bold_ref, dst_ref=bext.at[core, pl.ds(0, t_rows)],
        send_sem=bold_sem.at[1], recv_sem=bold_sem.at[2],
        device_id=at(flip=True), device_id_type=MESH,
    )
    for copy in halos + [share]:
        copy.start()

    runs_copy.wait()
    own_runs = runs_ref[:, pl.ds(pl.multiple_of(j * t_rows, LANES), t_rows)]
    next_runs = runs_ref[:, pl.ds(pl.multiple_of(lax.rem(j + 1, n_t) * t_rows, LANES), LANES)]
    runs = jnp.broadcast_to(jnp.concatenate([own_runs, next_runs], 1), (8, ext))
    end = jnp.where(j == n_t - 1, t_rows, ext)
    inside = iota((8, ext), 1) < end
    for m in range(1, MAXD + 1):
        same = (pltpu.roll(runs, m, 1) == runs) & inside
        masks[m - 1] = jnp.where(same, 1.0, 0.0)

    pl.semaphore_wait(near_sem, len(along))
    for where in (at(dz=-4), at(dz=4)):
        signal(far_sem, where)

    delays_copy.wait()
    shape = (8 * MAXD, n_rows)
    lag = iota(shape, 0) // 8 + 1
    delay_of = iota(shape, 1) // p_local
    right_p = iota(shape, 0) % p_local == iota(shape, 1) % p_local
    wanted = jnp.zeros(shape, jnp.int32)
    for k in range(DELAYS):
        wanted = jnp.where(delay_of == k, delays_ref[k], wanted)
    pick = jnp.where(right_p & (wanted == lag), 1.0, 0.0).astype(BF16)
    pick = jnp.concatenate([pick, pick], 1)

    for copy in hid_copies:
        copy.wait()
    nt = ((1,), (1,))
    g = dot(wbuf[j], hid[j], nt)
    for s in (1, 3, 2):
        w_sends[s - 1].wait_recv()
        source = lax.rem(j + n_t - s, n_t)
        g = g + dot(wbuf[source], hid[source], nt)

    high = g.astype(BF16)
    low = (g - high.astype(F32)).astype(BF16)
    lagged = dot(pick, jnp.concatenate([high, low], 0))
    lagged = jnp.concatenate([lagged, jnp.zeros((8 * MAXD, LANES), F32)], 1)
    gs = jnp.zeros((8, ext), F32)
    for m in range(1, MAXD + 1):
        gs = gs + pltpu.roll(lagged[8 * (m - 1):8 * m], m, 1) * masks[m - 1]

    second = jnp.concatenate([gs[:, HALF:], jnp.zeros((8, 2 * HALF - ext), F32)], 1)
    low_rows = iota((8, HALF), 0) < p_local
    abuf[f] = jnp.where(low_rows, gs[:, :HALF], second).astype(BF16)
    pl.semaphore_wait(far_sem, 2)
    a_sends = [remote(abuf.at[f], abuf.at[f], a_sem, s - 1, at(dz=N_ZLO * s)) for s in (2, 1, 3)]
    for copy in a_sends:
        copy.start()
    for copy in a_sends:
        copy.wait_recv()
    total = abuf[0].astype(F32)
    for s in range(1, n_f):
        total = total + abuf[s].astype(F32)
    xbuf[chip] = total.astype(BF16)

    steps = [(dx, dz) for dx in (2, 1, 3, 0) for dz in (-2, -1, 1, 0) if dx or dz]
    for dx, dz in steps:
        pltpu.make_async_remote_copy(
            src_ref=xbuf.at[chip], dst_ref=xbuf.at[chip],
            send_sem=x_sem.at[0], recv_sem=x_sem.at[1],
            device_id=at(dx=dx, dz=dz), device_id_type=MESH,
        ).start()
    for copy in halos + [share]:
        copy.wait_recv()
    bold_copy.wait()
    arrived = xbuf.at[pl.ds(0, n_v // 2 - 1)]
    pltpu.make_async_copy(arrived, arrived, x_sem.at[1]).wait()

    sums = xbuf[...].reshape(n_v // 2 * 8, HALF)
    halves = []
    for h in range(2):
        both = jnp.concatenate([bext[c, pl.ds(h * HALF, HALF), :] for c in range(2)], 1)
        halves.append(dot(sums, both))
    upper = iota((8, 2 * LANES), 0) < p_local
    for g2 in range(n_v // 4):
        a, b = slice(16 * g2, 16 * g2 + 8), slice(16 * g2 + 8, 16 * g2 + 16)
        u = jnp.where(upper, halves[0][a], halves[1][b])
        w = jnp.where(upper, halves[0][b], halves[1][a])
        r = (u + pltpu.roll(w, 4, 0)).astype(BF16)
        for c in range(2):
            sbuf[c, pl.ds(8 * g2, 8), :] = r[:, c * LANES:(c + 1) * LANES]
    rbuf[j, core] = sbuf[core]
    r_sends = []
    for n, (s, w) in enumerate(((2, True), (2, False), (1, True), (3, True), (1, False), (3, False), (0, True))):
        r_sends.append(
            remote(sbuf.at[1 - core if w else core], rbuf.at[j, core], r_sem, n, at(dj=s, flip=w))
        )
    for copy in r_sends:
        copy.start()
    for copy in r_sends:
        copy.wait_recv()
    upper = iota((8, LANES), 0) < p_local
    parts = []
    for c in range(2):
        r = rbuf[0, c].astype(F32)
        for s in range(1, n_t):
            r = r + rbuf[s, c].astype(F32)
        parts.append(r)
    for g2 in range(n_v // 4):
        v0, v1 = parts[0][8 * g2:8 * g2 + 8], parts[1][8 * g2:8 * g2 + 8]
        out_ref[pl.ds(16 * g2, 8), :] = jnp.where(upper, v0, pltpu.roll(v1, 4, 0))
        out_ref[pl.ds(16 * g2 + 8, 8), :] = jnp.where(upper, pltpu.roll(v0, 4, 0), v1)

    for copy in w_sends + a_sends + r_sends + halos + [share]:
        copy.wait_send()
    pltpu.make_async_copy(arrived, arrived, x_sem.at[0]).wait()


def shards(hidden, bold, panel, eigvals, ridge_grid, delays, runs):
    n_v, n_f, n_t = (lax.axis_size(axis) for axis in ("voxel", "feature", "tm"))
    t_rows, d_local = hidden.shape
    v_cols = bold.shape[1]
    p_local = panel.shape[1]
    n_p = n_v * p_local
    ext = t_rows + LANES
    d_chunk = d_local // n_t
    vmem = pl.BlockSpec(memory_space=pltpu.VMEM)
    hbm = pl.BlockSpec(memory_space=pl.ANY)
    dma = pltpu.SemaphoreType.DMA
    rotated = pl.pallas_call(
        functools.partial(kernel, (n_v, n_f, n_t, t_rows, d_local, p_local)),
        out_shape=jax.ShapeDtypeStruct((n_p, v_cols), F32),
        in_specs=[hbm] * 5,
        out_specs=vmem,
        scratch_shapes=[
            pltpu.SMEM((DELAYS,), jnp.int32),
            pltpu.VMEM((p_local, panel.shape[0]), BF16),
            pltpu.VMEM((1, runs.shape[0]), jnp.int32),
            pltpu.VMEM((n_t, t_rows, d_chunk), BF16),
            pltpu.VMEM((2, 2 * HALF, v_cols), BF16),
            pltpu.VMEM((n_t, DELAYS * p_local, d_chunk), BF16),
            pltpu.VMEM((n_f, 8, HALF), BF16),
            pltpu.VMEM((n_v // 2, 8, HALF), BF16),
            pltpu.VMEM((2, n_v * 2, v_cols), BF16),
            pltpu.VMEM((n_t, 2, n_v * 2, v_cols), BF16),
            pltpu.VMEM((MAXD, 8, ext), F32),
            dma((3,)),
            dma((n_t,)),
            dma((3,)),
            dma((2, 2)),
            dma((2, n_t - 1)),
            dma((2, n_f - 1)),
            dma((2,)),
            dma((2, 2 * n_t - 1)),
            pltpu.SemaphoreType.REGULAR,
            pltpu.SemaphoreType.REGULAR,
        ],
        compiler_params=pltpu.CompilerParams(collective_id=0, has_side_effects=True),
        name="sweep",
    )(delays, hidden, bold, panel.T, runs[None])
    penalty = 2.0 ** ((ridge_grid.astype(F32) - 8.0) * 0.5)
    scaled = rotated[None] / (
        math.sqrt(t_rows * n_t) * (eigvals[None, :, None] + penalty[:, None, None])
    )
    return scaled.astype(BF16)


def solution(mesh):
    return jax.shard_map(
        shards,
        mesh=mesh,
        in_specs=(
            P("tm", "feature"),
            P("tm", "voxel"),
            P(("feature", "tm"), "voxel"),
            P(),
            P(),
            P(),
            P(),
        ),
        out_specs=P(None, None, "voxel"),
        check_vma=False,
    )
```

```python
import functools
import math

import jax
import jax.numpy as jnp
from jax import lax
from jax.experimental import pallas as pl
from jax.experimental.pallas import tpu as pltpu
from jax.sharding import PartitionSpec as P

DELAYS = 8
MAXD = 12
RIDGES = 24
LANES = 128
HALF = 512
N_ZLO = 4
BF16 = jnp.bfloat16
F32 = jnp.float32
MESH = pl.DeviceIdType.MESH


def iota(shape, dim):
    return lax.broadcasted_iota(jnp.int32, shape, dim)


def dot(left, right, dims=((1,), (0,))):
    return lax.dot_general(left, right, (dims, ((), ())), preferred_element_type=F32)


def kernel(
    sizes,
    delays_hbm, ridge_hbm, hidden_ref, bold_ref, panel_hbm, runs_hbm, eig_hbm,
    out_ref,
    delays_ref, ridge_ref, panel_ref, runs_ref, eig_ref, scale,
    hid, bext, wbuf, abuf, xbuf, sbuf, rbuf, masks,
    in_sem, hid_sem, bold_sem, halo_sem, w_sem, a_sem, x_sem, r_sem, near_sem, far_sem,
):
    n_v, n_f, n_t, t_rows, d_local, p_local = sizes
    d_chunk = d_local // n_t
    ext = t_rows + LANES
    n_z = n_f * N_ZLO
    n_x = n_v // (2 * N_ZLO)
    i = lax.axis_index("voxel")
    f = lax.axis_index("feature")
    j = lax.axis_index("tm")
    core = lax.rem(i, 2)
    x = i // (2 * N_ZLO)
    z = f * N_ZLO + lax.rem(i // 2, N_ZLO)
    chip = i // 2

    def at(dx=0, dz=0, dj=0, flip=False):
        xx = lax.rem(x + dx, n_x)
        zz = lax.rem(z + dz + n_z, n_z)
        cc = 1 - core if flip else core
        return {
            "voxel": (xx * N_ZLO + lax.rem(zz, N_ZLO)) * 2 + cc,
            "feature": zz // N_ZLO,
            "tm": lax.rem(j + dj, n_t),
        }

    def signal(sem, where):
        pl.semaphore_signal(sem, inc=1, device_id=where, device_id_type=MESH)

    barrier = pltpu.get_barrier_semaphore()
    near = [at(dj=s, flip=w) for s in range(n_t) for w in (False, True) if s or w]
    near += [at(dx=s) for s in range(1, n_x)]
    along = [at(dz=s) for s in (-2, -1, 1, 2)]
    for where in near + along:
        signal(barrier, where)

    panel_copy = pltpu.make_async_copy(panel_hbm, panel_ref, in_sem.at[0])
    runs_copy = pltpu.make_async_copy(runs_hbm, runs_ref, in_sem.at[1])
    delays_copy = pltpu.make_async_copy(delays_hbm, delays_ref, in_sem.at[2])
    panel_copy.start()
    runs_copy.start()
    delays_copy.start()
    ridge_copy = pltpu.make_async_copy(ridge_hbm, ridge_ref, in_sem.at[3])
    eig_copy = pltpu.make_async_copy(eig_hbm, eig_ref, in_sem.at[4])
    ridge_copy.start()
    eig_copy.start()
    hid_copies = [
        pltpu.make_async_copy(
            hidden_ref.at[:, pl.ds(c * d_chunk, d_chunk)], hid.at[c], hid_sem.at[c]
        )
        for c in range(n_t)
    ]
    for copy in hid_copies:
        copy.start()
    bold_copy = pltpu.make_async_copy(bold_ref, bext.at[core, pl.ds(0, t_rows)], bold_sem.at[0])
    bold_copy.start()

    rows_local = panel_ref.shape[1]
    n_rows = DELAYS * p_local
    block = DELAYS * LANES
    spread = (iota((n_rows, p_local), 0) % p_local == iota((n_rows, p_local), 1)).astype(BF16)
    squeeze = (iota((block, LANES), 0) // DELAYS == iota((block, LANES), 1)).astype(BF16)
    keep = iota((n_rows, rows_local), 1) % DELAYS == iota((n_rows, rows_local), 0) // p_local
    panel_copy.wait()
    tall = dot(spread, panel_ref[...])
    tall = jnp.where(keep, tall, 0.0).astype(BF16)
    for b in range(rows_local // block):
        part = dot(tall[:, b * block:(b + 1) * block], squeeze)
        wbuf[j, :, pl.ds(b * LANES, LANES)] = part.astype(BF16)

    pl.semaphore_wait(barrier, len(near) + len(along))

    def remote(src, dst, sems, slot, where):
        return pltpu.make_async_remote_copy(
            src_ref=src, dst_ref=dst, send_sem=sems.at[0, slot], recv_sem=sems.at[1, slot],
            device_id=where, device_id_type=MESH,
        )

    w_sends = [remote(wbuf.at[j], wbuf.at[j], w_sem, s - 1, at(dj=s)) for s in range(1, n_t)]
    for copy in w_sends:
        copy.start()
    for where in along:
        signal(near_sem, where)
    tail = HALF * 2 - t_rows - 16
    for c in range(2):
        bext[c, pl.ds(t_rows + 16, tail), :] = jnp.zeros((tail, LANES), BF16)
    halos = [
        remote(
            bold_ref.at[pl.ds(0, 16)], bext.at[core, pl.ds(t_rows, 16)],
            halo_sem, s, at(dj=n_t - 1, flip=s == 1),
        )
        for s in range(2)
    ]
    share = pltpu.make_async_remote_copy(
        src_ref=bold_ref, dst_ref=bext.at[core, pl.ds(0, t_rows)],
        send_sem=bold_sem.at[1], recv_sem=bold_sem.at[2],
        device_id=at(flip=True), device_id_type=MESH,
    )
    for copy in halos + [share]:
        copy.start()

    runs_copy.wait()
    own_runs = runs_ref[:, pl.ds(pl.multiple_of(j * t_rows, LANES), t_rows)]
    next_runs = runs_ref[:, pl.ds(pl.multiple_of(lax.rem(j + 1, n_t) * t_rows, LANES), LANES)]
    runs = jnp.broadcast_to(jnp.concatenate([own_runs, next_runs], 1), (8, ext))
    end = jnp.where(j == n_t - 1, t_rows, ext)
    inside = iota((8, ext), 1) < end
    for m in range(1, MAXD + 1):
        same = (pltpu.roll(runs, m, 1) == runs) & inside
        masks[m - 1] = jnp.where(same, 1.0, 0.0)

    pl.semaphore_wait(near_sem, len(along))
    for where in (at(dz=-4), at(dz=4)):
        signal(far_sem, where)

    delays_copy.wait()
    shape = (8 * MAXD, n_rows)
    lag = iota(shape, 0) // 8 + 1
    delay_of = iota(shape, 1) // p_local
    right_p = iota(shape, 0) % p_local == iota(shape, 1) % p_local
    wanted = jnp.zeros(shape, jnp.int32)
    for k in range(DELAYS):
        wanted = jnp.where(delay_of == k, delays_ref[k], wanted)
    pick = jnp.where(right_p & (wanted == lag), 1.0, 0.0).astype(BF16)
    pick = jnp.concatenate([pick, pick], 1)

    for copy in hid_copies:
        copy.wait()
    nt = ((1,), (1,))
    g = dot(wbuf[j], hid[j], nt)
    for s in (1, 3, 2):
        w_sends[s - 1].wait_recv()
        source = lax.rem(j + n_t - s, n_t)
        g = g + dot(wbuf[source], hid[source], nt)

    high = g.astype(BF16)
    low = (g - high.astype(F32)).astype(BF16)
    lagged = dot(pick, jnp.concatenate([high, low], 0))
    lagged = jnp.concatenate([lagged, jnp.zeros((8 * MAXD, LANES), F32)], 1)
    gs = jnp.zeros((8, ext), F32)
    for m in range(1, MAXD + 1):
        gs = gs + pltpu.roll(lagged[8 * (m - 1):8 * m], m, 1) * masks[m - 1]

    second = jnp.concatenate([gs[:, HALF:], jnp.zeros((8, 2 * HALF - ext), F32)], 1)
    low_rows = iota((8, HALF), 0) < p_local
    abuf[f] = jnp.where(low_rows, gs[:, :HALF], second).astype(BF16)
    pl.semaphore_wait(far_sem, 2)
    a_sends = [remote(abuf.at[f], abuf.at[f], a_sem, s - 1, at(dz=N_ZLO * s)) for s in (2, 1, 3)]
    for copy in a_sends:
        copy.start()

    ridge_copy.wait()
    eig_copy.wait()
    n_p = eig_ref.shape[1]
    eig = jnp.broadcast_to(eig_ref[...], (LANES, n_p)).T

    def factor(n, carry):
        level = jnp.full((8, LANES), ridge_ref[n], jnp.int32).astype(F32)
        penalty = jnp.exp2((level - 8.0) * 0.5)
        whole_penalty = jnp.concatenate([penalty] * (n_p // 8), 0)
        scale[n] = 1.0 / (math.sqrt(t_rows * n_t) * (eig + whole_penalty))
        return carry

    lax.fori_loop(0, RIDGES, factor, 0)
    for copy in a_sends:
        copy.wait_recv()
    total = abuf[0].astype(F32)
    for s in range(1, n_f):
        total = total + abuf[s].astype(F32)
    xbuf[chip] = total.astype(BF16)

    steps = [(dx, dz) for dx in (2, 1, 3, 0) for dz in (-2, -1, 1, 0) if dx or dz]
    for dx, dz in steps:
        pltpu.make_async_remote_copy(
            src_ref=xbuf.at[chip], dst_ref=xbuf.at[chip],
            send_sem=x_sem.at[0], recv_sem=x_sem.at[1],
            device_id=at(dx=dx, dz=dz), device_id_type=MESH,
        ).start()
    for copy in halos + [share]:
        copy.wait_recv()
    bold_copy.wait()
    arrived = xbuf.at[pl.ds(0, n_v // 2 - 1)]
    pltpu.make_async_copy(arrived, arrived, x_sem.at[1]).wait()

    sums = xbuf[...].reshape(n_v // 2 * 8, HALF)
    halves = []
    for h in range(2):
        both = jnp.concatenate([bext[c, pl.ds(h * HALF, HALF), :] for c in range(2)], 1)
        halves.append(dot(sums, both))
    upper = iota((8, 2 * LANES), 0) < p_local
    for g2 in range(n_v // 4):
        a, b = slice(16 * g2, 16 * g2 + 8), slice(16 * g2 + 8, 16 * g2 + 16)
        u = jnp.where(upper, halves[0][a], halves[1][b])
        w = jnp.where(upper, halves[0][b], halves[1][a])
        r = (u + pltpu.roll(w, 4, 0)).astype(BF16)
        for c in range(2):
            sbuf[c, pl.ds(8 * g2, 8), :] = r[:, c * LANES:(c + 1) * LANES]
    rbuf[j, core] = sbuf[core]
    r_sends = []
    for n, (s, w) in enumerate(((2, True), (2, False), (1, True), (3, True), (1, False), (3, False), (0, True))):
        r_sends.append(
            remote(sbuf.at[1 - core if w else core], rbuf.at[j, core], r_sem, n, at(dj=s, flip=w))
        )
    for copy in r_sends:
        copy.start()
    for copy in r_sends:
        copy.wait_recv()
    upper = iota((8, LANES), 0) < p_local
    parts = []
    for c in range(2):
        r = rbuf[0, c].astype(F32)
        for s in range(1, n_t):
            r = r + rbuf[s, c].astype(F32)
        parts.append(r)
    tiles = []
    for g2 in range(n_v // 4):
        v0, v1 = parts[0][8 * g2:8 * g2 + 8], parts[1][8 * g2:8 * g2 + 8]
        tiles.append(jnp.where(upper, v0, pltpu.roll(v1, 4, 0)))
        tiles.append(jnp.where(upper, pltpu.roll(v0, 4, 0), v1))
    rotated = jnp.concatenate(tiles, 0)
    for n in range(RIDGES):
        out_ref[n] = (rotated * scale[n]).astype(BF16)

    for copy in w_sends + a_sends + r_sends + halos + [share]:
        copy.wait_send()
    pltpu.make_async_copy(arrived, arrived, x_sem.at[0]).wait()


def shards(hidden, bold, panel, eigvals, ridge_grid, delays, runs):
    n_v, n_f, n_t = (lax.axis_size(axis) for axis in ("voxel", "feature", "tm"))
    t_rows, d_local = hidden.shape
    v_cols = bold.shape[1]
    p_local = panel.shape[1]
    n_p = n_v * p_local
    ext = t_rows + LANES
    d_chunk = d_local // n_t
    hbm = pl.BlockSpec(memory_space=pl.ANY)
    dma = pltpu.SemaphoreType.DMA
    return pl.pallas_call(
        functools.partial(kernel, (n_v, n_f, n_t, t_rows, d_local, p_local)),
        out_shape=pltpu.VMEM((RIDGES, n_p, v_cols), BF16),
        in_specs=[hbm] * 7,
        out_specs=pl.BlockSpec(memory_space=pltpu.VMEM),
        scratch_shapes=[
            pltpu.SMEM((DELAYS,), jnp.int32),
            pltpu.SMEM((RIDGES,), jnp.int32),
            pltpu.VMEM((p_local, panel.shape[0]), BF16),
            pltpu.VMEM((1, runs.shape[0]), jnp.int32),
            pltpu.VMEM((1, n_p), F32),
            pltpu.VMEM((RIDGES, n_p, v_cols), F32),
            pltpu.VMEM((n_t, t_rows, d_chunk), BF16),
            pltpu.VMEM((2, 2 * HALF, v_cols), BF16),
            pltpu.VMEM((n_t, DELAYS * p_local, d_chunk), BF16),
            pltpu.VMEM((n_f, 8, HALF), BF16),
            pltpu.VMEM((n_v // 2, 8, HALF), BF16),
            pltpu.VMEM((2, n_v * 2, v_cols), BF16),
            pltpu.VMEM((n_t, 2, n_v * 2, v_cols), BF16),
            pltpu.VMEM((MAXD, 8, ext), F32),
            dma((5,)),
            dma((n_t,)),
            dma((3,)),
            dma((2, 2)),
            dma((2, n_t - 1)),
            dma((2, n_f - 1)),
            dma((2,)),
            dma((2, 2 * n_t - 1)),
            pltpu.SemaphoreType.REGULAR,
            pltpu.SemaphoreType.REGULAR,
        ],
        compiler_params=pltpu.CompilerParams(collective_id=0, has_side_effects=True),
        name="sweep",
    )(delays, ridge_grid, hidden, bold, panel.T, runs[None], eigvals[None])


def solution(mesh):
    return jax.shard_map(
        shards,
        mesh=mesh,
        in_specs=(
            P("tm", "feature"),
            P("tm", "voxel"),
            P(("feature", "tm"), "voxel"),
            P(),
            P(),
            P(),
            P(),
        ),
        out_specs=P(None, None, "voxel"),
        check_vma=False,
    )
```

```python
import functools
import math

import jax
import jax.numpy as jnp
from jax import lax
from jax.experimental import pallas as pl
from jax.experimental.pallas import tpu as pltpu
from jax.sharding import PartitionSpec as P

DELAYS = 8
MAXD = 12
RIDGES = 24
LANES = 128
HALF = 512
N_ZLO = 4
BF16 = jnp.bfloat16
F32 = jnp.float32
MESH = pl.DeviceIdType.MESH


def iota(shape, dim):
    return lax.broadcasted_iota(jnp.int32, shape, dim)


def dot(left, right, dims=((1,), (0,))):
    return lax.dot_general(left, right, (dims, ((), ())), preferred_element_type=F32)


def kernel(
    sizes,
    delays_hbm, ridge_hbm, hidden_ref, bold_ref, panel_hbm, runs_hbm, eig_hbm,
    out_ref,
    delays_ref, ridge_ref, panel_ref, runs_ref, eig_ref, scale,
    hid, bext, wbuf, abuf, xbuf, sbuf, rbuf, masks,
    in_sem, hid_sem, bold_sem, halo_sem, w_sem, a_sem, x_sem, r_sem, near_sem, chain_sem,
):
    n_v, n_f, n_t, t_rows, d_local, p_local = sizes
    d_chunk = d_local // n_t
    ext = t_rows + LANES
    n_z = n_f * N_ZLO
    n_x = n_v // (2 * N_ZLO)
    i = lax.axis_index("voxel")
    f = lax.axis_index("feature")
    j = lax.axis_index("tm")
    core = lax.rem(i, 2)
    x = i // (2 * N_ZLO)
    z = f * N_ZLO + lax.rem(i // 2, N_ZLO)
    chip = i // 2

    def at(dx=0, dz=0, dj=0, flip=False):
        xx = lax.rem(x + dx, n_x)
        zz = lax.rem(z + dz + n_z, n_z)
        cc = 1 - core if flip else core
        return {
            "voxel": (xx * N_ZLO + lax.rem(zz, N_ZLO)) * 2 + cc,
            "feature": zz // N_ZLO,
            "tm": lax.rem(j + dj, n_t),
        }

    def signal(sem, where):
        pl.semaphore_signal(sem, inc=1, device_id=where, device_id_type=MESH)

    barrier = pltpu.get_barrier_semaphore()
    sibling = at(flip=True)
    tm_peers = {step: at(dj=step) for step in range(1, n_t)}
    x_peers = [at(dx=step) for step in range(1, n_x)]
    along = {step: at(dz=step) for step in (-2, -1, 1, 2)}
    near = [*tm_peers.values(), *along.values(), *x_peers, sibling]
    for where in near:
        signal(barrier, where)

    panel_copy = pltpu.make_async_copy(panel_hbm, panel_ref, in_sem.at[0])
    runs_copy = pltpu.make_async_copy(runs_hbm, runs_ref, in_sem.at[1])
    delays_copy = pltpu.make_async_copy(delays_hbm, delays_ref, in_sem.at[2])
    panel_copy.start()
    runs_copy.start()
    delays_copy.start()
    ridge_copy = pltpu.make_async_copy(ridge_hbm, ridge_ref, in_sem.at[3])
    eig_copy = pltpu.make_async_copy(eig_hbm, eig_ref, in_sem.at[4])
    ridge_copy.start()
    eig_copy.start()
    hid_copies = [
        pltpu.make_async_copy(
            hidden_ref.at[:, pl.ds(c * d_chunk, d_chunk)], hid.at[c], hid_sem.at[c]
        )
        for c in range(n_t)
    ]
    for copy in hid_copies:
        copy.start()
    bold_copy = pltpu.make_async_copy(bold_ref, bext.at[core, pl.ds(0, t_rows)], bold_sem.at[0])
    bold_copy.start()

    rows_local = panel_ref.shape[1]
    n_rows = DELAYS * p_local
    block = DELAYS * LANES
    spread = (iota((n_rows, p_local), 0) % p_local == iota((n_rows, p_local), 1)).astype(BF16)
    squeeze = (iota((block, LANES), 0) // DELAYS == iota((block, LANES), 1)).astype(BF16)
    keep = iota((n_rows, rows_local), 1) % DELAYS == iota((n_rows, rows_local), 0) // p_local
    panel_copy.wait()
    tall = dot(spread, panel_ref[...])
    tall = jnp.where(keep, tall, 0.0).astype(BF16)
    for b in range(rows_local // block):
        part = dot(tall[:, b * block:(b + 1) * block], squeeze)
        wbuf[j, :, pl.ds(b * LANES, LANES)] = part.astype(BF16)

    other_tm_peers = {step: at(dj=step, flip=True) for step in range(1, n_t)}
    z_peers = {step: at(dz=N_ZLO * step) for step in range(1, n_f)}
    window = [
        at(dx=dx, dz=dz) for dx in (2, 1, 3, 0) for dz in (-2, -1, 1, 0) if dx or dz
    ]

    pl.semaphore_wait(barrier, len(near))

    def remote(src, dst, sems, slot, where):
        return pltpu.make_async_remote_copy(
            src_ref=src, dst_ref=dst, send_sem=sems.at[0, slot], recv_sem=sems.at[1, slot],
            device_id=where, device_id_type=MESH,
        )

    w_sends = {s: remote(wbuf.at[j], wbuf.at[j], w_sem, s - 1, tm_peers[s]) for s in (2, 1, 3)}
    for copy in w_sends.values():
        copy.start()
    signal(chain_sem.at[0], along[2])
    for where in (*along.values(), sibling):
        signal(near_sem, where)
    tail = HALF * 2 - t_rows - 16
    for c in range(2):
        bext[c, pl.ds(t_rows + 16, tail), :] = jnp.zeros((tail, LANES), BF16)
    halos = [
        remote(
            bold_ref.at[pl.ds(0, 16)], bext.at[core, pl.ds(t_rows, 16)],
            halo_sem, s, (other_tm_peers if s else tm_peers)[n_t - 1],
        )
        for s in range(2)
    ]
    share = pltpu.make_async_remote_copy(
        src_ref=bold_ref, dst_ref=bext.at[core, pl.ds(0, t_rows)],
        send_sem=bold_sem.at[1], recv_sem=bold_sem.at[2],
        device_id=sibling, device_id_type=MESH,
    )
    halos[0].start()
    share.start()

    runs_copy.wait()
    own_runs = runs_ref[:, pl.ds(pl.multiple_of(j * t_rows, LANES), t_rows)]
    next_runs = runs_ref[:, pl.ds(pl.multiple_of(lax.rem(j + 1, n_t) * t_rows, LANES), LANES)]
    runs = jnp.broadcast_to(jnp.concatenate([own_runs, next_runs], 1), (8, ext))
    end = jnp.where(j == n_t - 1, t_rows, ext)
    inside = iota((8, ext), 1) < end
    for m in range(1, MAXD + 1):
        same = (pltpu.roll(runs, m, 1) == runs) & inside
        masks[m - 1] = jnp.where(same, 1.0, 0.0)

    pl.semaphore_wait(chain_sem.at[0], 1)
    signal(chain_sem.at[1], along[2])

    delays_copy.wait()
    shape = (8 * MAXD, n_rows)
    lag = iota(shape, 0) // 8 + 1
    delay_of = iota(shape, 1) // p_local
    right_p = iota(shape, 0) % p_local == iota(shape, 1) % p_local
    wanted = jnp.zeros(shape, jnp.int32)
    for k in range(DELAYS):
        wanted = jnp.where(delay_of == k, delays_ref[k], wanted)
    pick = jnp.where(right_p & (wanted == lag), 1.0, 0.0).astype(BF16)
    pick = jnp.concatenate([pick, pick], 1)

    for copy in hid_copies:
        copy.wait()
    nt = ((1,), (1,))
    g = dot(wbuf[j], hid[j], nt)
    for s in (1, 3, 2):
        if s == 2:
            pl.semaphore_wait(chain_sem.at[1], 1)
            signal(chain_sem.at[2], along[2])
        w_sends[s].wait_recv()
        source = lax.rem(j + n_t - s, n_t)
        g = g + dot(wbuf[source], hid[source], nt)

    high = g.astype(BF16)
    low = (g - high.astype(F32)).astype(BF16)
    lagged = dot(pick, jnp.concatenate([high, low], 0))
    lagged = jnp.concatenate([lagged, jnp.zeros((8 * MAXD, LANES), F32)], 1)
    gs = jnp.zeros((8, ext), F32)
    for m in range(1, MAXD + 1):
        gs = gs + pltpu.roll(lagged[8 * (m - 1):8 * m], m, 1) * masks[m - 1]

    second = jnp.concatenate([gs[:, HALF:], jnp.zeros((8, 2 * HALF - ext), F32)], 1)
    low_rows = iota((8, HALF), 0) < p_local
    abuf[f] = jnp.where(low_rows, gs[:, :HALF], second).astype(BF16)
    a_sends = {s: remote(abuf.at[f], abuf.at[f], a_sem, s - 1, z_peers[s]) for s in (1, 3, 2)}
    pl.semaphore_wait(near_sem, len(along) + 1)
    a_sends[1].start()
    a_sends[3].start()
    pl.semaphore_wait(chain_sem.at[2], 1)
    a_sends[2].start()
    halos[1].start()

    ridge_copy.wait()
    eig_copy.wait()
    n_p = eig_ref.shape[1]
    eig = jnp.broadcast_to(eig_ref[...], (LANES, n_p)).T

    def factor(n, carry):
        level = jnp.full((8, LANES), ridge_ref[n], jnp.int32).astype(F32)
        penalty = jnp.exp2((level - 8.0) * 0.5)
        whole_penalty = jnp.concatenate([penalty] * (n_p // 8), 0)
        scale[n] = 1.0 / (math.sqrt(t_rows * n_t) * (eig + whole_penalty))
        return carry

    lax.fori_loop(0, RIDGES, factor, 0)
    for copy in a_sends.values():
        copy.wait_recv()
    total = abuf[0].astype(F32)
    for s in range(1, n_f):
        total = total + abuf[s].astype(F32)
    xbuf[chip] = total.astype(BF16)

    for where in window:
        pltpu.make_async_remote_copy(
            src_ref=xbuf.at[chip], dst_ref=xbuf.at[chip],
            send_sem=x_sem.at[0], recv_sem=x_sem.at[1],
            device_id=where, device_id_type=MESH,
        ).start()
    for copy in halos + [share]:
        copy.wait_recv()
    bold_copy.wait()
    arrived = xbuf.at[pl.ds(0, n_v // 2 - 1)]
    pltpu.make_async_copy(arrived, arrived, x_sem.at[1]).wait()

    sums = xbuf[...].reshape(n_v // 2 * 8, HALF)
    halves = []
    for h in range(2):
        both = jnp.concatenate([bext[c, pl.ds(h * HALF, HALF), :] for c in range(2)], 1)
        halves.append(dot(sums, both))
    upper = iota((8, 2 * LANES), 0) < p_local
    for g2 in range(n_v // 4):
        a, b = slice(16 * g2, 16 * g2 + 8), slice(16 * g2 + 8, 16 * g2 + 16)
        u = jnp.where(upper, halves[0][a], halves[1][b])
        w = jnp.where(upper, halves[0][b], halves[1][a])
        r = (u + pltpu.roll(w, 4, 0)).astype(BF16)
        for c in range(2):
            sbuf[c, pl.ds(8 * g2, 8), :] = r[:, c * LANES:(c + 1) * LANES]
    rbuf[j, core] = sbuf[core]
    order = [(2, 1), (2, 0), (1, 1), (3, 1), (1, 0), (3, 0), (0, 1)]
    r_sends = []
    for n, (s, w) in enumerate(order):
        where = sibling if s == 0 else (other_tm_peers if w else tm_peers)[s]
        r_sends.append(remote(sbuf.at[1 - core if w else core], rbuf.at[j, core], r_sem, n, where))
    for copy in r_sends:
        copy.start()
    for copy in r_sends:
        copy.wait_recv()
    upper = iota((8, LANES), 0) < p_local
    parts = []
    for c in range(2):
        r = rbuf[0, c].astype(F32)
        for s in range(1, n_t):
            r = r + rbuf[s, c].astype(F32)
        parts.append(r)
    tiles = []
    for g2 in range(n_v // 4):
        v0, v1 = parts[0][8 * g2:8 * g2 + 8], parts[1][8 * g2:8 * g2 + 8]
        tiles.append(jnp.where(upper, v0, pltpu.roll(v1, 4, 0)))
        tiles.append(jnp.where(upper, pltpu.roll(v0, 4, 0), v1))
    rotated = jnp.concatenate(tiles, 0)
    for n in range(RIDGES):
        out_ref[n] = (rotated * scale[n]).astype(BF16)

    for copy in [*w_sends.values(), *a_sends.values(), *r_sends, *halos, share]:
        copy.wait_send()
    pltpu.make_async_copy(arrived, arrived, x_sem.at[0]).wait()


def shards(hidden, bold, panel, eigvals, ridge_grid, delays, runs):
    n_v, n_f, n_t = (lax.axis_size(axis) for axis in ("voxel", "feature", "tm"))
    t_rows, d_local = hidden.shape
    v_cols = bold.shape[1]
    p_local = panel.shape[1]
    n_p = n_v * p_local
    ext = t_rows + LANES
    d_chunk = d_local // n_t
    hbm = pl.BlockSpec(memory_space=pl.ANY)
    dma = pltpu.SemaphoreType.DMA
    return pl.pallas_call(
        functools.partial(kernel, (n_v, n_f, n_t, t_rows, d_local, p_local)),
        out_shape=pltpu.VMEM((RIDGES, n_p, v_cols), BF16),
        in_specs=[hbm] * 7,
        out_specs=pl.BlockSpec(memory_space=pltpu.VMEM),
        scratch_shapes=[
            pltpu.SMEM((DELAYS,), jnp.int32),
            pltpu.SMEM((RIDGES,), jnp.int32),
            pltpu.VMEM((p_local, panel.shape[0]), BF16),
            pltpu.VMEM((1, runs.shape[0]), jnp.int32),
            pltpu.VMEM((1, n_p), F32),
            pltpu.VMEM((RIDGES, n_p, v_cols), F32),
            pltpu.VMEM((n_t, t_rows, d_chunk), BF16),
            pltpu.VMEM((2, 2 * HALF, v_cols), BF16),
            pltpu.VMEM((n_t, DELAYS * p_local, d_chunk), BF16),
            pltpu.VMEM((n_f, 8, HALF), BF16),
            pltpu.VMEM((n_v // 2, 8, HALF), BF16),
            pltpu.VMEM((2, n_v * 2, v_cols), BF16),
            pltpu.VMEM((n_t, 2, n_v * 2, v_cols), BF16),
            pltpu.VMEM((MAXD, 8, ext), F32),
            dma((5,)),
            dma((n_t,)),
            dma((3,)),
            dma((2, 2)),
            dma((2, n_t - 1)),
            dma((2, n_f - 1)),
            dma((2,)),
            dma((2, 2 * n_t - 1)),
            pltpu.SemaphoreType.REGULAR,
            pltpu.SemaphoreType.REGULAR((3,)),
        ],
        compiler_params=pltpu.CompilerParams(collective_id=0, has_side_effects=True),
        name="sweep",
    )(delays, ridge_grid, hidden, bold, panel.T, runs[None], eigvals[None])


def solution(mesh):
    return jax.shard_map(
        shards,
        mesh=mesh,
        in_specs=(
            P("tm", "feature"),
            P("tm", "voxel"),
            P(("feature", "tm"), "voxel"),
            P(),
            P(),
            P(),
            P(),
        ),
        out_specs=P(None, None, "voxel"),
        check_vma=False,
    )
```

```python
import functools
import math

import jax
import jax.numpy as jnp
from jax import lax
from jax.experimental import pallas as pl
from jax.experimental.pallas import tpu as pltpu
from jax.sharding import PartitionSpec as P

DELAYS = 8
MAXD = 12
RIDGES = 24
LANES = 128
HALF = 512
N_ZLO = 4
BF16 = jnp.bfloat16
F32 = jnp.float32
MESH = pl.DeviceIdType.MESH


def iota(shape, dim):
    return lax.broadcasted_iota(jnp.int32, shape, dim)


def dot(left, right, dims=((1,), (0,))):
    return lax.dot_general(left, right, (dims, ((), ())), preferred_element_type=F32)


def kernel(
    sizes,
    delays_hbm, ridge_hbm, hidden_ref, bold_ref, panel_hbm, runs_hbm, eig_hbm,
    out_ref,
    delays_ref, ridge_ref, panel_ref, runs_ref, eig_ref, scale,
    hid, bext, wbuf, gbuf, abuf, xbuf, sbuf, rbuf, masks,
    in_sem, hid_sem, bold_sem, halo_sem, w_sem, a_sem, x_sem, r_sem, near_sem, far_sem,
):
    n_v, n_f, n_t, t_rows, d_local, p_local = sizes
    d_chunk = d_local // n_t
    ext = t_rows + LANES
    n_z = n_f * N_ZLO
    n_x = n_v // (2 * N_ZLO)
    i = lax.axis_index("voxel")
    f = lax.axis_index("feature")
    j = lax.axis_index("tm")
    core = lax.rem(i, 2)
    x = i // (2 * N_ZLO)
    z = f * N_ZLO + lax.rem(i // 2, N_ZLO)
    chip = x * N_ZLO + lax.rem(z + 2, N_ZLO)

    def at(dx=0, dz=0, dj=0, flip=False):
        xx = lax.rem(x + dx, n_x)
        zz = lax.rem(z + dz + n_z, n_z)
        cc = 1 - core if flip else core
        return {
            "voxel": (xx * N_ZLO + lax.rem(zz, N_ZLO)) * 2 + cc,
            "feature": zz // N_ZLO,
            "tm": lax.rem(j + dj, n_t),
        }

    def signal(sem, where):
        pl.semaphore_signal(sem, inc=1, device_id=where, device_id_type=MESH)

    barrier = pltpu.get_barrier_semaphore()
    tm_peers, along = {}, {}
    for step in (2, 1, 3):
        tm_peers[step] = at(dj=step)
        signal(barrier, tm_peers[step])
    for step in (2, -2, 1, -1):
        along[step] = at(dz=step)
        signal(barrier, along[step])
    sibling = at(flip=True)
    signal(barrier, sibling)
    for step in range(1, n_x):
        signal(barrier, at(dx=step))

    panel_copy = pltpu.make_async_copy(panel_hbm, panel_ref, in_sem.at[0])
    runs_copy = pltpu.make_async_copy(runs_hbm, runs_ref, in_sem.at[1])
    delays_copy = pltpu.make_async_copy(delays_hbm, delays_ref, in_sem.at[2])
    panel_copy.start()
    runs_copy.start()
    delays_copy.start()
    ridge_copy = pltpu.make_async_copy(ridge_hbm, ridge_ref, in_sem.at[3])
    eig_copy = pltpu.make_async_copy(eig_hbm, eig_ref, in_sem.at[4])
    ridge_copy.start()
    eig_copy.start()
    hid_copies = [
        pltpu.make_async_copy(
            hidden_ref.at[:, pl.ds(c * d_chunk, d_chunk)], hid.at[c], hid_sem.at[c]
        )
        for c in range(n_t)
    ]
    for copy in hid_copies:
        copy.start()
    bold_copy = pltpu.make_async_copy(bold_ref, bext.at[core, pl.ds(0, t_rows)], bold_sem.at[0])
    bold_copy.start()

    rows_local = panel_ref.shape[1]
    n_rows = DELAYS * p_local
    block = DELAYS * LANES
    spread = (iota((n_rows, p_local), 0) % p_local == iota((n_rows, p_local), 1)).astype(BF16)
    squeeze = (iota((block, LANES), 0) // DELAYS == iota((block, LANES), 1)).astype(BF16)
    keep = iota((n_rows, rows_local), 1) % DELAYS == iota((n_rows, rows_local), 0) // p_local
    panel_copy.wait()
    tall = dot(spread, panel_ref[...])
    tall = jnp.where(keep, tall, 0.0).astype(BF16)
    for b in range(rows_local // block):
        part = dot(tall[:, b * block:(b + 1) * block], squeeze)
        wbuf[j, :, pl.ds(b * LANES, LANES)] = part.astype(BF16)

    other_tm_peers = {step: at(dj=step, flip=True) for step in range(1, n_t)}
    z_peers = {step: along[step] if step in along else at(dz=step) for step in (6, -6, 2, -2)}
    window = [
        at(dx=dx, dz=dz) for dx in (2, 1, 3, 0) for dz in (-2, -1, 1, 0) if dx or dz
    ]

    pl.semaphore_wait(barrier, len(tm_peers) + len(along) + n_x)

    def remote(src, dst, sems, slot, where):
        return pltpu.make_async_remote_copy(
            src_ref=src, dst_ref=dst, send_sem=sems.at[0, slot], recv_sem=sems.at[1, slot],
            device_id=where, device_id_type=MESH,
        )

    w_sends = {s: remote(wbuf.at[j], wbuf.at[j], w_sem, s - 1, tm_peers[s]) for s in (2, 1, 3)}
    for copy in w_sends.values():
        copy.start()
    for where in (*along.values(), sibling):
        signal(near_sem, where)
    tail = HALF * 2 - t_rows - 16
    for c in range(2):
        bext[c, pl.ds(t_rows + 16, tail), :] = jnp.zeros((tail, LANES), BF16)
    halos = [
        remote(
            bold_ref.at[pl.ds(0, 16)], bext.at[core, pl.ds(t_rows, 16)],
            halo_sem, s, (other_tm_peers if s else tm_peers)[n_t - 1],
        )
        for s in range(2)
    ]
    share = pltpu.make_async_remote_copy(
        src_ref=bold_ref, dst_ref=bext.at[core, pl.ds(0, t_rows)],
        send_sem=bold_sem.at[1], recv_sem=bold_sem.at[2],
        device_id=sibling, device_id_type=MESH,
    )
    halos[0].start()
    share.start()

    runs_copy.wait()
    own_runs = runs_ref[:, pl.ds(pl.multiple_of(j * t_rows, LANES), t_rows)]
    next_runs = runs_ref[:, pl.ds(pl.multiple_of(lax.rem(j + 1, n_t) * t_rows, LANES), LANES)]
    runs = jnp.broadcast_to(jnp.concatenate([own_runs, next_runs], 1), (8, ext))
    end = jnp.where(j == n_t - 1, t_rows, ext)
    inside = iota((8, ext), 1) < end
    for m in range(1, MAXD + 1):
        same = (pltpu.roll(runs, m, 1) == runs) & inside
        masks[m - 1] = jnp.where(same, 1.0, 0.0)

    pl.semaphore_wait(near_sem, len(along) + 1)
    signal(far_sem, along[2])
    signal(far_sem, along[-2])

    delays_copy.wait()
    shape = (8 * MAXD, n_rows)
    lag = iota(shape, 0) // 8 + 1
    delay_of = iota(shape, 1) // p_local
    right_p = iota(shape, 0) % p_local == iota(shape, 1) % p_local
    wanted = jnp.zeros(shape, jnp.int32)
    for k in range(DELAYS):
        wanted = jnp.where(delay_of == k, delays_ref[k], wanted)
    pick = jnp.where(right_p & (wanted == lag), 1.0, 0.0).astype(BF16)
    pick = jnp.concatenate([pick, pick], 1)

    for copy in hid_copies:
        copy.wait()
    nt = ((1,), (1,))
    g = dot(wbuf[j], hid[j], nt)
    for s in (1, 3, 2):
        w_sends[s].wait_recv()
        source = lax.rem(j + n_t - s, n_t)
        g = g + dot(wbuf[source], hid[source], nt)

    high = g.astype(BF16)
    low = (g - high.astype(F32)).astype(BF16)
    lagged = dot(pick, jnp.concatenate([high, low], 0))
    lagged = jnp.concatenate([lagged, jnp.zeros((8 * MAXD, LANES), F32)], 1)
    gs = jnp.zeros((8, ext), F32)
    for m in range(1, MAXD + 1):
        gs = gs + pltpu.roll(lagged[8 * (m - 1):8 * m], m, 1) * masks[m - 1]

    second = jnp.concatenate([gs[:, HALF:], jnp.zeros((8, 2 * HALF - ext), F32)], 1)
    low_rows = iota((8, HALF), 0) < p_local
    gbuf[...] = jnp.where(low_rows, gs[:, :HALF], second).astype(BF16)
    a_sends = [
        remote(gbuf, abuf.at[f], a_sem, n, where) for n, where in enumerate(z_peers.values())
    ]
    pl.semaphore_wait(far_sem, 2)
    for copy in a_sends:
        copy.start()
    halos[1].start()

    ridge_copy.wait()
    eig_copy.wait()
    n_p = eig_ref.shape[1]
    eig = jnp.broadcast_to(eig_ref[...], (LANES, n_p)).T

    def factor(n, carry):
        level = jnp.full((8, LANES), ridge_ref[n], jnp.int32).astype(F32)
        penalty = jnp.exp2((level - 8.0) * 0.5)
        whole_penalty = jnp.concatenate([penalty] * (n_p // 8), 0)
        scale[n] = 1.0 / (math.sqrt(t_rows * n_t) * (eig + whole_penalty))
        return carry

    lax.fori_loop(0, RIDGES, factor, 0)
    for copy in a_sends:
        copy.wait_recv()
    total = abuf[0].astype(F32)
    for s in range(1, n_f):
        total = total + abuf[s].astype(F32)
    xbuf[chip] = total.astype(BF16)

    for where in window:
        pltpu.make_async_remote_copy(
            src_ref=xbuf.at[chip], dst_ref=xbuf.at[chip],
            send_sem=x_sem.at[0], recv_sem=x_sem.at[1],
            device_id=where, device_id_type=MESH,
        ).start()
    for copy in halos + [share]:
        copy.wait_recv()
    bold_copy.wait()
    arrived = xbuf.at[pl.ds(0, n_v // 2 - 1)]
    pltpu.make_async_copy(arrived, arrived, x_sem.at[1]).wait()

    sums = xbuf[...].reshape(n_v // 2 * 8, HALF)
    halves = []
    for h in range(2):
        both = jnp.concatenate([bext[c, pl.ds(h * HALF, HALF), :] for c in range(2)], 1)
        halves.append(dot(sums, both))
    upper = iota((8, 2 * LANES), 0) < p_local
    for g2 in range(n_v // 4):
        a, b = slice(16 * g2, 16 * g2 + 8), slice(16 * g2 + 8, 16 * g2 + 16)
        u = jnp.where(upper, halves[0][a], halves[1][b])
        w = jnp.where(upper, halves[0][b], halves[1][a])
        r = (u + pltpu.roll(w, 4, 0)).astype(BF16)
        for c in range(2):
            sbuf[c, pl.ds(8 * g2, 8), :] = r[:, c * LANES:(c + 1) * LANES]
    rbuf[j, core] = sbuf[core]
    order = [(2, 1), (2, 0), (1, 1), (3, 1), (1, 0), (3, 0), (0, 1)]
    r_sends = []
    for n, (s, w) in enumerate(order):
        where = sibling if s == 0 else (other_tm_peers if w else tm_peers)[s]
        r_sends.append(remote(sbuf.at[1 - core if w else core], rbuf.at[j, core], r_sem, n, where))
    for copy in r_sends:
        copy.start()
    for copy in r_sends:
        copy.wait_recv()
    upper = iota((8, LANES), 0) < p_local
    parts = []
    for c in range(2):
        r = rbuf[0, c].astype(F32)
        for s in range(1, n_t):
            r = r + rbuf[s, c].astype(F32)
        parts.append(r)
    tiles = []
    for g2 in range(n_v // 4):
        v0, v1 = parts[0][8 * g2:8 * g2 + 8], parts[1][8 * g2:8 * g2 + 8]
        tiles.append(jnp.where(upper, v0, pltpu.roll(v1, 4, 0)))
        tiles.append(jnp.where(upper, pltpu.roll(v0, 4, 0), v1))
    rotated = jnp.concatenate(tiles, 0)
    for n in range(RIDGES):
        out_ref[n] = (rotated * scale[n]).astype(BF16)

    for copy in [*w_sends.values(), *a_sends, *r_sends, *halos, share]:
        copy.wait_send()
    pltpu.make_async_copy(arrived, arrived, x_sem.at[0]).wait()


def shards(hidden, bold, panel, eigvals, ridge_grid, delays, runs):
    n_v, n_f, n_t = (lax.axis_size(axis) for axis in ("voxel", "feature", "tm"))
    t_rows, d_local = hidden.shape
    v_cols = bold.shape[1]
    p_local = panel.shape[1]
    n_p = n_v * p_local
    ext = t_rows + LANES
    d_chunk = d_local // n_t
    hbm = pl.BlockSpec(memory_space=pl.ANY)
    dma = pltpu.SemaphoreType.DMA
    return pl.pallas_call(
        functools.partial(kernel, (n_v, n_f, n_t, t_rows, d_local, p_local)),
        out_shape=pltpu.VMEM((RIDGES, n_p, v_cols), BF16),
        in_specs=[hbm] * 7,
        out_specs=pl.BlockSpec(memory_space=pltpu.VMEM),
        scratch_shapes=[
            pltpu.SMEM((DELAYS,), jnp.int32),
            pltpu.SMEM((RIDGES,), jnp.int32),
            pltpu.VMEM((p_local, panel.shape[0]), BF16),
            pltpu.VMEM((1, runs.shape[0]), jnp.int32),
            pltpu.VMEM((1, n_p), F32),
            pltpu.VMEM((RIDGES, n_p, v_cols), F32),
            pltpu.VMEM((n_t, t_rows, d_chunk), BF16),
            pltpu.VMEM((2, 2 * HALF, v_cols), BF16),
            pltpu.VMEM((n_t, DELAYS * p_local, d_chunk), BF16),
            pltpu.VMEM((8, HALF), BF16),
            pltpu.VMEM((n_f, 8, HALF), BF16),
            pltpu.VMEM((n_v // 2, 8, HALF), BF16),
            pltpu.VMEM((2, n_v * 2, v_cols), BF16),
            pltpu.VMEM((n_t, 2, n_v * 2, v_cols), BF16),
            pltpu.VMEM((MAXD, 8, ext), F32),
            dma((5,)),
            dma((n_t,)),
            dma((3,)),
            dma((2, 2)),
            dma((2, n_t - 1)),
            dma((2, n_f)),
            dma((2,)),
            dma((2, 2 * n_t - 1)),
            pltpu.SemaphoreType.REGULAR,
            pltpu.SemaphoreType.REGULAR,
        ],
        compiler_params=pltpu.CompilerParams(collective_id=0, has_side_effects=True),
        name="sweep",
    )(delays, ridge_grid, hidden, bold, panel.T, runs[None], eigvals[None])


def solution(mesh):
    return jax.shard_map(
        shards,
        mesh=mesh,
        in_specs=(
            P("tm", "feature"),
            P("tm", "voxel"),
            P(("feature", "tm"), "voxel"),
            P(),
            P(),
            P(),
            P(),
        ),
        out_specs=P(None, None, "voxel"),
        check_vma=False,
    )
```

```python
import functools
import math

import jax
import jax.numpy as jnp
from jax import lax
from jax.experimental import pallas as pl
from jax.experimental.pallas import tpu as pltpu
from jax.sharding import PartitionSpec as P

DELAYS = 8
MAXD = 12
RIDGES = 24
LANES = 128
HALF = 512
N_ZLO = 4
COLUMNS = (0, 1, 3, 2)
BF16 = jnp.bfloat16
F32 = jnp.float32
MESH = pl.DeviceIdType.MESH


def iota(shape, dim):
    return lax.broadcasted_iota(jnp.int32, shape, dim)


def dot(left, right, dims=((1,), (0,))):
    return lax.dot_general(left, right, (dims, ((), ())), preferred_element_type=F32)


def kernel(
    sizes,
    delays_hbm, ridge_hbm, hidden_ref, bold_ref, panel_hbm, runs_hbm, eig_hbm,
    out_ref,
    delays_ref, ridge_ref, panel_ref, runs_ref, eig_ref, scale,
    hid, bext, wbuf, gbuf, abuf, xbuf, sbuf, rbuf, masks,
    in_sem, hid_sem, bold_sem, halo_sem, w_sem, a_sem, x_sem, r_sem, near_sem, far_sem,
):
    n_v, n_f, n_t, t_rows, d_local, p_local = sizes
    d_chunk = d_local // n_t
    ext = t_rows + LANES
    n_z = n_f * N_ZLO
    n_x = n_v // (2 * N_ZLO)
    i = lax.axis_index("voxel")
    f = lax.axis_index("feature")
    j = lax.axis_index("tm")
    core = lax.rem(i, 2)
    x = i // (2 * N_ZLO)
    z = f * N_ZLO + lax.rem(i // 2, N_ZLO)
    z_sum = lax.rem(z + 2, N_ZLO)

    def at(dx=0, dz=0, dj=0, flip=False):
        xx = lax.rem(x + dx, n_x)
        zz = lax.rem(z + dz + n_z, n_z)
        cc = 1 - core if flip else core
        return {
            "voxel": (xx * N_ZLO + lax.rem(zz, N_ZLO)) * 2 + cc,
            "feature": zz // N_ZLO,
            "tm": lax.rem(j + dj, n_t),
        }

    def signal(sem, where):
        pl.semaphore_signal(sem, inc=1, device_id=where, device_id_type=MESH)

    barrier = pltpu.get_barrier_semaphore()
    tm_peers, along = {}, {}
    for step in (2, 1, 3):
        tm_peers[step] = at(dj=step)
        signal(barrier, tm_peers[step])
    for step in (2, -2, 1, -1):
        along[step] = at(dz=step)
        signal(barrier, along[step])
    sibling = at(flip=True)
    signal(barrier, sibling)
    for step in range(1, n_x):
        signal(barrier, at(dx=step))

    panel_copy = pltpu.make_async_copy(panel_hbm, panel_ref, in_sem.at[0])
    runs_copy = pltpu.make_async_copy(runs_hbm, runs_ref, in_sem.at[1])
    delays_copy = pltpu.make_async_copy(delays_hbm, delays_ref, in_sem.at[2])
    panel_copy.start()
    runs_copy.start()
    delays_copy.start()
    ridge_copy = pltpu.make_async_copy(ridge_hbm, ridge_ref, in_sem.at[3])
    eig_copy = pltpu.make_async_copy(eig_hbm, eig_ref, in_sem.at[4])
    ridge_copy.start()
    eig_copy.start()
    hid_copies = [
        pltpu.make_async_copy(
            hidden_ref.at[:, pl.ds(c * d_chunk, d_chunk)], hid.at[c], hid_sem.at[c]
        )
        for c in range(n_t)
    ]
    for copy in hid_copies:
        copy.start()
    bold_copy = pltpu.make_async_copy(bold_ref, bext.at[core, pl.ds(0, t_rows)], bold_sem.at[0])
    bold_copy.start()

    rows_local = panel_ref.shape[1]
    n_rows = DELAYS * p_local
    block = DELAYS * LANES
    spread = (iota((n_rows, p_local), 0) % p_local == iota((n_rows, p_local), 1)).astype(BF16)
    squeeze = (iota((block, LANES), 0) // DELAYS == iota((block, LANES), 1)).astype(BF16)
    keep = iota((n_rows, rows_local), 1) % DELAYS == iota((n_rows, rows_local), 0) // p_local
    panel_copy.wait()
    tall = dot(spread, panel_ref[...])
    tall = jnp.where(keep, tall, 0.0).astype(BF16)
    for b in range(rows_local // block):
        part = dot(tall[:, b * block:(b + 1) * block], squeeze)
        wbuf[j, :, pl.ds(b * LANES, LANES)] = part.astype(BF16)

    other_tm_peers = {step: at(dj=step, flip=True) for step in range(1, n_t)}
    z_peers = {step: along[step] if step in along else at(dz=step) for step in (6, -6, 2, -2)}
    window = [
        (COLUMNS.index((n_x - dx) % n_x), at(dx=dx, dz=dz))
        for dx in (2, 1, 3, 0) for dz in (-2, -1, 1, 0) if dx or dz
    ]

    pl.semaphore_wait(barrier, len(tm_peers) + len(along) + n_x)

    def remote(src, dst, sems, slot, where):
        return pltpu.make_async_remote_copy(
            src_ref=src, dst_ref=dst, send_sem=sems.at[0, slot], recv_sem=sems.at[1, slot],
            device_id=where, device_id_type=MESH,
        )

    w_sends = {s: remote(wbuf.at[j], wbuf.at[j], w_sem, s - 1, tm_peers[s]) for s in (2, 1, 3)}
    for copy in w_sends.values():
        copy.start()
    for where in (*along.values(), sibling):
        signal(near_sem, where)
    tail = HALF * 2 - t_rows - 16
    for c in range(2):
        bext[c, pl.ds(t_rows + 16, tail), :] = jnp.zeros((tail, LANES), BF16)
    halos = [
        remote(
            bold_ref.at[pl.ds(0, 16)], bext.at[core, pl.ds(t_rows, 16)],
            halo_sem, s, (other_tm_peers if s else tm_peers)[n_t - 1],
        )
        for s in range(2)
    ]
    share = pltpu.make_async_remote_copy(
        src_ref=bold_ref, dst_ref=bext.at[core, pl.ds(0, t_rows)],
        send_sem=bold_sem.at[1], recv_sem=bold_sem.at[2],
        device_id=sibling, device_id_type=MESH,
    )
    halos[0].start()
    share.start()

    runs_copy.wait()
    own_runs = runs_ref[:, pl.ds(pl.multiple_of(j * t_rows, LANES), t_rows)]
    next_runs = runs_ref[:, pl.ds(pl.multiple_of(lax.rem(j + 1, n_t) * t_rows, LANES), LANES)]
    runs = jnp.broadcast_to(jnp.concatenate([own_runs, next_runs], 1), (8, ext))
    end = jnp.where(j == n_t - 1, t_rows, ext)
    inside = iota((8, ext), 1) < end
    for m in range(1, MAXD + 1):
        same = (pltpu.roll(runs, m, 1) == runs) & inside
        masks[m - 1] = jnp.where(same, 1.0, 0.0)

    pl.semaphore_wait(near_sem, len(along) + 1)
    signal(far_sem, along[2])
    signal(far_sem, along[-2])

    delays_copy.wait()
    shape = (8 * MAXD, n_rows)
    lag = iota(shape, 0) // 8 + 1
    delay_of = iota(shape, 1) // p_local
    right_p = iota(shape, 0) % p_local == iota(shape, 1) % p_local
    wanted = jnp.zeros(shape, jnp.int32)
    for k in range(DELAYS):
        wanted = jnp.where(delay_of == k, delays_ref[k], wanted)
    pick = jnp.where(right_p & (wanted == lag), 1.0, 0.0).astype(BF16)
    pick = jnp.concatenate([pick, pick], 1)

    for copy in hid_copies:
        copy.wait()
    nt = ((1,), (1,))
    g = dot(wbuf[j], hid[j], nt)
    for s in (1, 3, 2):
        w_sends[s].wait_recv()
        source = lax.rem(j + n_t - s, n_t)
        g = g + dot(wbuf[source], hid[source], nt)

    high = g.astype(BF16)
    low = (g - high.astype(F32)).astype(BF16)
    lagged = dot(pick, jnp.concatenate([high, low], 0))
    lagged = jnp.concatenate([lagged, jnp.zeros((8 * MAXD, LANES), F32)], 1)
    gs = jnp.zeros((8, ext), F32)
    for m in range(1, MAXD + 1):
        gs = gs + pltpu.roll(lagged[8 * (m - 1):8 * m], m, 1) * masks[m - 1]

    second = jnp.concatenate([gs[:, HALF:], jnp.zeros((8, 2 * HALF - ext), F32)], 1)
    low_rows = iota((8, HALF), 0) < p_local
    gbuf[...] = jnp.where(low_rows, gs[:, :HALF], second).astype(BF16)
    a_sends = [
        remote(gbuf, abuf.at[f], a_sem, n, where) for n, where in enumerate(z_peers.values())
    ]
    pl.semaphore_wait(far_sem, 2)
    for copy in a_sends:
        copy.start()
    halos[1].start()

    ridge_copy.wait()
    eig_copy.wait()
    n_p = eig_ref.shape[1]
    eig = jnp.broadcast_to(eig_ref[...], (LANES, n_p)).T

    def factor(n, carry):
        level = jnp.full((8, LANES), ridge_ref[n], jnp.int32).astype(F32)
        penalty = jnp.exp2((level - 8.0) * 0.5)
        whole_penalty = jnp.concatenate([penalty] * (n_p // 8), 0)
        scale[n] = 1.0 / (math.sqrt(t_rows * n_t) * (eig + whole_penalty))
        return carry

    lax.fori_loop(0, RIDGES, factor, 0)
    for copy in a_sends:
        copy.wait_recv()
    total = abuf[0].astype(F32)
    for s in range(1, n_f):
        total = total + abuf[s].astype(F32)
    xbuf[z_sum] = total.astype(BF16)

    early = N_ZLO * (n_x - 1)
    for column, where in window:
        pltpu.make_async_remote_copy(
            src_ref=xbuf.at[z_sum], dst_ref=xbuf.at[column * N_ZLO + z_sum],
            send_sem=x_sem.at[0], recv_sem=x_sem.at[1 if column < n_x - 1 else 2],
            device_id=where, device_id_type=MESH,
        ).start()
    for copy in halos + [share]:
        copy.wait_recv()
    bold_copy.wait()

    halves = [
        jnp.concatenate([bext[c, pl.ds(h * HALF, HALF), :] for c in range(2)], 1) for h in range(2)
    ]
    order = [(2, 1), (2, 0), (1, 1), (3, 1), (1, 0), (3, 0), (0, 1)]

    def multiply_and_send(first, count, slot):
        sums = xbuf[first:first + count].reshape(count * 8, HALF)
        both = [dot(sums, half) for half in halves]
        upper = iota((8, 2 * LANES), 0) < p_local
        for g2 in range(count // 2):
            a, b = slice(16 * g2, 16 * g2 + 8), slice(16 * g2 + 8, 16 * g2 + 16)
            u = jnp.where(upper, both[0][a], both[1][b])
            w = jnp.where(upper, both[0][b], both[1][a])
            r = (u + pltpu.roll(w, 4, 0)).astype(BF16)
            for c in range(2):
                sbuf[c, pl.ds(4 * first + 8 * g2, 8), :] = r[:, c * LANES:(c + 1) * LANES]
        rows = pl.ds(4 * first, 4 * count)
        copies = []
        for n, (s, w) in enumerate(order):
            where = sibling if s == 0 else (other_tm_peers if w else tm_peers)[s]
            copies.append(
                remote(
                    sbuf.at[1 - core if w else core, rows], rbuf.at[j, core, rows],
                    r_sem, slot + n, where,
                )
            )
        for copy in copies:
            copy.start()
        rbuf[j, core, rows] = sbuf[core, rows]
        return copies

    arrived = xbuf.at[pl.ds(0, early - 1)]
    pltpu.make_async_copy(arrived, arrived, x_sem.at[1]).wait()
    r_sends = multiply_and_send(0, early, 0)
    arrived = xbuf.at[pl.ds(0, N_ZLO)]
    pltpu.make_async_copy(arrived, arrived, x_sem.at[2]).wait()
    last_sends = multiply_and_send(early, N_ZLO, len(order))

    def finish(copies, first, columns):
        for copy in copies:
            copy.wait_recv()
        upper = iota((8, LANES), 0) < p_local
        for q in range(first, first + columns):
            parts = []
            for c in range(2):
                rows = pl.ds(16 * q, 16)
                r = rbuf[0, c, rows].astype(F32)
                for s in range(1, n_t):
                    r = r + rbuf[s, c, rows].astype(F32)
                parts.append(r)
            tiles = []
            for g2 in range(2):
                v0, v1 = parts[0][8 * g2:8 * g2 + 8], parts[1][8 * g2:8 * g2 + 8]
                tiles.append(jnp.where(upper, v0, pltpu.roll(v1, 4, 0)))
                tiles.append(jnp.where(upper, pltpu.roll(v0, 4, 0), v1))
            rotated = jnp.concatenate(tiles, 0)
            span = pl.ds(pl.multiple_of(lax.rem(x + COLUMNS[q], n_x) * 32, 32), 32)
            for n in range(RIDGES):
                out_ref[n, span, :] = (rotated * scale[n, span, :]).astype(BF16)

    finish(r_sends, 0, n_x - 1)
    finish(last_sends, n_x - 1, 1)

    for copy in [*w_sends.values(), *a_sends, *r_sends, *last_sends, *halos, share]:
        copy.wait_send()
    sent = xbuf.at[pl.ds(0, n_v // 2 - 1)]
    pltpu.make_async_copy(sent, sent, x_sem.at[0]).wait()


def shards(hidden, bold, panel, eigvals, ridge_grid, delays, runs):
    n_v, n_f, n_t = (lax.axis_size(axis) for axis in ("voxel", "feature", "tm"))
    t_rows, d_local = hidden.shape
    v_cols = bold.shape[1]
    p_local = panel.shape[1]
    n_p = n_v * p_local
    ext = t_rows + LANES
    d_chunk = d_local // n_t
    hbm = pl.BlockSpec(memory_space=pl.ANY)
    dma = pltpu.SemaphoreType.DMA
    return pl.pallas_call(
        functools.partial(kernel, (n_v, n_f, n_t, t_rows, d_local, p_local)),
        out_shape=pltpu.VMEM((RIDGES, n_p, v_cols), BF16),
        in_specs=[hbm] * 7,
        out_specs=pl.BlockSpec(memory_space=pltpu.VMEM),
        scratch_shapes=[
            pltpu.SMEM((DELAYS,), jnp.int32),
            pltpu.SMEM((RIDGES,), jnp.int32),
            pltpu.VMEM((p_local, panel.shape[0]), BF16),
            pltpu.VMEM((1, runs.shape[0]), jnp.int32),
            pltpu.VMEM((1, n_p), F32),
            pltpu.VMEM((RIDGES, n_p, v_cols), F32),
            pltpu.VMEM((n_t, t_rows, d_chunk), BF16),
            pltpu.VMEM((2, 2 * HALF, v_cols), BF16),
            pltpu.VMEM((n_t, DELAYS * p_local, d_chunk), BF16),
            pltpu.VMEM((8, HALF), BF16),
            pltpu.VMEM((n_f, 8, HALF), BF16),
            pltpu.VMEM((n_v // 2, 8, HALF), BF16),
            pltpu.VMEM((2, n_v * 2, v_cols), BF16),
            pltpu.VMEM((n_t, 2, n_v * 2, v_cols), BF16),
            pltpu.VMEM((MAXD, 8, ext), F32),
            dma((5,)),
            dma((n_t,)),
            dma((3,)),
            dma((2, 2)),
            dma((2, n_t - 1)),
            dma((2, n_f)),
            dma((3,)),
            dma((2, 4 * n_t - 2)),
            pltpu.SemaphoreType.REGULAR,
            pltpu.SemaphoreType.REGULAR,
        ],
        compiler_params=pltpu.CompilerParams(collective_id=0, has_side_effects=True),
        name="sweep",
    )(delays, ridge_grid, hidden, bold, panel.T, runs[None], eigvals[None])


def solution(mesh):
    return jax.shard_map(
        shards,
        mesh=mesh,
        in_specs=(
            P("tm", "feature"),
            P("tm", "voxel"),
            P(("feature", "tm"), "voxel"),
            P(),
            P(),
            P(),
            P(),
        ),
        out_specs=P(None, None, "voxel"),
        check_vma=False,
    )
```

```python
import functools
import math

import jax
import jax.numpy as jnp
from jax import lax
from jax.experimental import pallas as pl
from jax.experimental.pallas import tpu as pltpu
from jax.sharding import PartitionSpec as P

DELAYS = 8
MAXD = 12
RIDGES = 24
LANES = 128
HALF = 512
N_ZLO = 4
BF16 = jnp.bfloat16
F32 = jnp.float32
MESH = pl.DeviceIdType.MESH


def iota(shape, dim):
    return lax.broadcasted_iota(jnp.int32, shape, dim)


def dot(left, right, dims=((1,), (0,))):
    return lax.dot_general(left, right, (dims, ((), ())), preferred_element_type=F32)


def kernel(
    sizes,
    delays_hbm, ridge_hbm, hidden_ref, bold_ref, panel_hbm, runs_hbm, eig_hbm,
    out_ref,
    delays_ref, ridge_ref, panel_ref, runs_ref, eig_ref, scale,
    hid, bext, wbuf, gbuf, abuf, xbuf, rbuf, masks,
    in_sem, hid_sem, bold_sem, halo_sem, w_sem, a_sem, x_sem, r_sem, near_sem, far_sem,
):
    n_v, n_f, n_t, t_rows, d_local, p_local = sizes
    d_chunk = d_local // n_t
    ext = t_rows + LANES
    n_z = n_f * N_ZLO
    n_x = n_v // (2 * N_ZLO)
    i = lax.axis_index("voxel")
    f = lax.axis_index("feature")
    j = lax.axis_index("tm")
    core = lax.rem(i, 2)
    x = i // (2 * N_ZLO)
    z = f * N_ZLO + lax.rem(i // 2, N_ZLO)
    group = (x * N_ZLO + lax.rem(z + 2, N_ZLO)) * 2 + core

    def at(dx=0, dz=0, dj=0, flip=False):
        xx = lax.rem(x + dx, n_x)
        zz = lax.rem(z + dz + n_z, n_z)
        cc = 1 - core if flip else core
        return {
            "voxel": (xx * N_ZLO + lax.rem(zz, N_ZLO)) * 2 + cc,
            "feature": zz // N_ZLO,
            "tm": lax.rem(j + dj, n_t),
        }

    def signal(sem, where):
        pl.semaphore_signal(sem, inc=1, device_id=where, device_id_type=MESH)

    barrier = pltpu.get_barrier_semaphore()
    tm_peers, along = {}, {}
    for step in (2, 1, 3):
        tm_peers[step] = at(dj=step)
        signal(barrier, tm_peers[step])
    for step in (2, -2, 1, -1):
        along[step] = at(dz=step)
        signal(barrier, along[step])
    sibling = at(flip=True)
    signal(barrier, sibling)
    for step in range(1, n_x):
        signal(barrier, at(dx=step))

    panel_copy = pltpu.make_async_copy(panel_hbm, panel_ref, in_sem.at[0])
    runs_copy = pltpu.make_async_copy(runs_hbm, runs_ref, in_sem.at[1])
    delays_copy = pltpu.make_async_copy(delays_hbm, delays_ref, in_sem.at[2])
    panel_copy.start()
    runs_copy.start()
    delays_copy.start()
    ridge_copy = pltpu.make_async_copy(ridge_hbm, ridge_ref, in_sem.at[3])
    eig_copy = pltpu.make_async_copy(eig_hbm, eig_ref, in_sem.at[4])
    ridge_copy.start()
    eig_copy.start()
    hid_copies = [
        pltpu.make_async_copy(
            hidden_ref.at[:, pl.ds(c * d_chunk, d_chunk)], hid.at[c], hid_sem.at[c]
        )
        for c in range(n_t)
    ]
    for copy in hid_copies:
        copy.start()
    bold_copy = pltpu.make_async_copy(bold_ref, bext.at[pl.ds(0, t_rows)], bold_sem)
    bold_copy.start()

    rows_local = panel_ref.shape[1]
    n_rows = DELAYS * p_local
    block = DELAYS * LANES
    spread = (iota((n_rows, p_local), 0) % p_local == iota((n_rows, p_local), 1)).astype(BF16)
    squeeze = (iota((block, LANES), 0) // DELAYS == iota((block, LANES), 1)).astype(BF16)
    keep = iota((n_rows, rows_local), 1) % DELAYS == iota((n_rows, rows_local), 0) // p_local
    panel_copy.wait()
    tall = dot(spread, panel_ref[...])
    tall = jnp.where(keep, tall, 0.0).astype(BF16)
    for b in range(rows_local // block):
        part = dot(tall[:, b * block:(b + 1) * block], squeeze)
        wbuf[j, :, pl.ds(b * LANES, LANES)] = part.astype(BF16)

    z_peers = {step: along[step] if step in along else at(dz=step) for step in (6, -6, 2, -2)}
    reach = [(dx, dz) for dx in range(n_x) for dz in (-2, -1, 0, 1)]
    reach.sort(key=lambda step: -min(step[0], n_x - step[0]) - abs(step[1]))
    window = [
        at(dx=dx, dz=dz, flip=flip) for dx, dz in reach for flip in (True, False) if dx or dz or flip
    ]

    pl.semaphore_wait(barrier, len(tm_peers) + len(along) + n_x)

    def remote(src, dst, sems, slot, where):
        return pltpu.make_async_remote_copy(
            src_ref=src, dst_ref=dst, send_sem=sems.at[0, slot], recv_sem=sems.at[1, slot],
            device_id=where, device_id_type=MESH,
        )

    w_sends = {s: remote(wbuf.at[j], wbuf.at[j], w_sem, s - 1, tm_peers[s]) for s in (2, 1, 3)}
    for copy in w_sends.values():
        copy.start()
    for where in (*along.values(), sibling):
        signal(near_sem, where)
    tail = HALF * 2 - t_rows - 16
    bext[pl.ds(t_rows + 16, tail), :] = jnp.zeros((tail, LANES), BF16)
    halo = remote(
        bold_ref.at[pl.ds(0, 16)], bext.at[pl.ds(t_rows, 16)], halo_sem, 0, tm_peers[n_t - 1]
    )
    halo.start()

    runs_copy.wait()
    own_runs = runs_ref[:, pl.ds(pl.multiple_of(j * t_rows, LANES), t_rows)]
    next_runs = runs_ref[:, pl.ds(pl.multiple_of(lax.rem(j + 1, n_t) * t_rows, LANES), LANES)]
    runs = jnp.broadcast_to(jnp.concatenate([own_runs, next_runs], 1), (8, ext))
    end = jnp.where(j == n_t - 1, t_rows, ext)
    inside = iota((8, ext), 1) < end
    for m in range(1, MAXD + 1):
        same = (pltpu.roll(runs, m, 1) == runs) & inside
        masks[m - 1] = jnp.where(same, 1.0, 0.0)

    pl.semaphore_wait(near_sem, len(along) + 1)
    signal(far_sem, along[2])
    signal(far_sem, along[-2])
    signal(far_sem, sibling)

    delays_copy.wait()
    shape = (8 * MAXD, n_rows)
    lag = iota(shape, 0) // 8 + 1
    delay_of = iota(shape, 1) // p_local
    right_p = iota(shape, 0) % p_local == iota(shape, 1) % p_local
    wanted = jnp.zeros(shape, jnp.int32)
    for k in range(DELAYS):
        wanted = jnp.where(delay_of == k, delays_ref[k], wanted)
    pick = jnp.where(right_p & (wanted == lag), 1.0, 0.0).astype(BF16)
    pick = jnp.concatenate([pick, pick], 1)

    for copy in hid_copies:
        copy.wait()
    nt = ((1,), (1,))
    g = dot(wbuf[j], hid[j], nt)
    for s in (1, 3, 2):
        w_sends[s].wait_recv()
        source = lax.rem(j + n_t - s, n_t)
        g = g + dot(wbuf[source], hid[source], nt)

    high = g.astype(BF16)
    low = (g - high.astype(F32)).astype(BF16)
    lagged = dot(pick, jnp.concatenate([high, low], 0))
    lagged = jnp.concatenate([lagged, jnp.zeros((8 * MAXD, LANES), F32)], 1)
    gs = jnp.zeros((8, ext), F32)
    for m in range(1, MAXD + 1):
        gs = gs + pltpu.roll(lagged[8 * (m - 1):8 * m], m, 1) * masks[m - 1]

    second = jnp.concatenate([gs[:, HALF:], jnp.zeros((8, 2 * HALF - ext), F32)], 1)
    low_rows = iota((8, HALF), 0) < p_local
    gbuf[...] = jnp.where(low_rows, gs[:, :HALF], second).astype(BF16)
    a_sends = [
        remote(gbuf, abuf.at[f], a_sem, n, where) for n, where in enumerate(z_peers.values())
    ]
    pl.semaphore_wait(far_sem, 3)
    for copy in a_sends:
        copy.start()

    ridge_copy.wait()
    eig_copy.wait()
    n_p = eig_ref.shape[1]
    eig = jnp.broadcast_to(eig_ref[...], (LANES, n_p)).T

    def factor(n, carry):
        level = jnp.full((8, LANES), ridge_ref[n], jnp.int32).astype(F32)
        penalty = jnp.exp2((level - 8.0) * 0.5)
        whole_penalty = jnp.concatenate([penalty] * (n_p // 8), 0)
        scale[n] = 1.0 / (math.sqrt(t_rows * n_t) * (eig + whole_penalty))
        return carry

    lax.fori_loop(0, RIDGES, factor, 0)
    for copy in a_sends:
        copy.wait_recv()
    total = abuf[0].astype(F32)
    for s in range(1, n_f):
        total = total + abuf[s].astype(F32)
    xbuf[group] = total.astype(BF16)

    for where in window:
        pltpu.make_async_remote_copy(
            src_ref=xbuf.at[group], dst_ref=xbuf.at[group],
            send_sem=x_sem.at[0], recv_sem=x_sem.at[1],
            device_id=where, device_id_type=MESH,
        ).start()
    halo.wait_recv()
    bold_copy.wait()
    arrived = xbuf.at[pl.ds(0, n_v - 1)]
    pltpu.make_async_copy(arrived, arrived, x_sem.at[1]).wait()

    sums = xbuf[...].reshape(n_v * 8, HALF)
    halves = [dot(sums, bext[pl.ds(h * HALF, HALF), :]) for h in range(2)]
    upper = iota((8, LANES), 0) < p_local
    for g2 in range(n_v // 2):
        a, b = slice(16 * g2, 16 * g2 + 8), slice(16 * g2 + 8, 16 * g2 + 16)
        u = jnp.where(upper, halves[0][a], halves[1][b])
        w = jnp.where(upper, halves[0][b], halves[1][a])
        rbuf[j, pl.ds(8 * g2, 8), :] = (u + pltpu.roll(w, 4, 0)).astype(BF16)
    r_sends = [remote(rbuf.at[j], rbuf.at[j], r_sem, s - 1, tm_peers[s]) for s in (2, 1, 3)]
    for copy in r_sends:
        copy.start()
    for copy in r_sends:
        copy.wait_recv()
    rotated = rbuf[0].astype(F32)
    for s in range(1, n_t):
        rotated = rotated + rbuf[s].astype(F32)
    for n in range(RIDGES):
        out_ref[n] = (rotated * scale[n]).astype(BF16)

    for copy in [*w_sends.values(), *a_sends, *r_sends, halo]:
        copy.wait_send()
    pltpu.make_async_copy(arrived, arrived, x_sem.at[0]).wait()


def shards(hidden, bold, panel, eigvals, ridge_grid, delays, runs):
    n_v, n_f, n_t = (lax.axis_size(axis) for axis in ("voxel", "feature", "tm"))
    t_rows, d_local = hidden.shape
    v_cols = bold.shape[1]
    p_local = panel.shape[1]
    n_p = n_v * p_local
    ext = t_rows + LANES
    d_chunk = d_local // n_t
    hbm = pl.BlockSpec(memory_space=pl.ANY)
    dma = pltpu.SemaphoreType.DMA
    return pl.pallas_call(
        functools.partial(kernel, (n_v, n_f, n_t, t_rows, d_local, p_local)),
        out_shape=pltpu.VMEM((RIDGES, n_p, v_cols), BF16),
        in_specs=[hbm] * 7,
        out_specs=pl.BlockSpec(memory_space=pltpu.VMEM),
        scratch_shapes=[
            pltpu.SMEM((DELAYS,), jnp.int32),
            pltpu.SMEM((RIDGES,), jnp.int32),
            pltpu.VMEM((p_local, panel.shape[0]), BF16),
            pltpu.VMEM((1, runs.shape[0]), jnp.int32),
            pltpu.VMEM((1, n_p), F32),
            pltpu.VMEM((RIDGES, n_p, v_cols), F32),
            pltpu.VMEM((n_t, t_rows, d_chunk), BF16),
            pltpu.VMEM((2 * HALF, v_cols), BF16),
            pltpu.VMEM((n_t, DELAYS * p_local, d_chunk), BF16),
            pltpu.VMEM((8, HALF), BF16),
            pltpu.VMEM((n_f, 8, HALF), BF16),
            pltpu.VMEM((n_v, 8, HALF), BF16),
            pltpu.VMEM((n_t, n_p, v_cols), BF16),
            pltpu.VMEM((MAXD, 8, ext), F32),
            dma((5,)),
            dma((n_t,)),
            dma,
            dma((2, 1)),
            dma((2, n_t - 1)),
            dma((2, n_f)),
            dma((2,)),
            dma((2, n_t - 1)),
            pltpu.SemaphoreType.REGULAR,
            pltpu.SemaphoreType.REGULAR,
        ],
        compiler_params=pltpu.CompilerParams(collective_id=0, has_side_effects=True),
        name="sweep",
    )(delays, ridge_grid, hidden, bold, panel.T, runs[None], eigvals[None])


def solution(mesh):
    return jax.shard_map(
        shards,
        mesh=mesh,
        in_specs=(
            P("tm", "feature"),
            P("tm", "voxel"),
            P(("feature", "tm"), "voxel"),
            P(),
            P(),
            P(),
            P(),
        ),
        out_specs=P(None, None, "voxel"),
        check_vma=False,
    )
```

```python
import functools
import math

import jax
import jax.numpy as jnp
from jax import lax
from jax.experimental import pallas as pl
from jax.experimental.pallas import tpu as pltpu
from jax.sharding import PartitionSpec as P

DELAYS = 8
MAXD = 12
RIDGES = 24
LANES = 128
HALF = 512
N_ZLO = 4
BF16 = jnp.bfloat16
F32 = jnp.float32
MESH = pl.DeviceIdType.MESH


def iota(shape, dim):
    return lax.broadcasted_iota(jnp.int32, shape, dim)


def dot(left, right, dims=((1,), (0,))):
    return lax.dot_general(left, right, (dims, ((), ())), preferred_element_type=F32)


def kernel(
    sizes,
    delays_hbm, ridge_hbm, hidden_ref, bold_ref, panel_hbm, runs_hbm, eig_hbm,
    out_ref,
    delays_ref, ridge_ref, panel_ref, runs_ref, eig_ref, scale,
    hid, bext, wbuf, gbuf, abuf, xbuf, rbuf, masks,
    in_sem, hid_sem, bold_sem, halo_sem, w_sem, a_sem, x_sem, r_sem, near_sem, far_sem,
):
    n_v, n_f, n_t, t_rows, d_local, p_local = sizes
    d_chunk = d_local // n_t
    ext = t_rows + LANES
    n_z = n_f * N_ZLO
    n_x = n_v // (2 * N_ZLO)
    i = lax.axis_index("voxel")
    f = lax.axis_index("feature")
    j = lax.axis_index("tm")
    core = lax.rem(i, 2)
    x = i // (2 * N_ZLO)
    z = f * N_ZLO + lax.rem(i // 2, N_ZLO)
    group = (x * N_ZLO + lax.rem(z + 2, N_ZLO)) * 2 + core

    def at(dx=0, dz=0, dj=0, flip=False):
        xx = lax.rem(x + dx, n_x)
        zz = lax.rem(z + dz + n_z, n_z)
        cc = 1 - core if flip else core
        return {
            "voxel": (xx * N_ZLO + lax.rem(zz, N_ZLO)) * 2 + cc,
            "feature": zz // N_ZLO,
            "tm": lax.rem(j + dj, n_t),
        }

    def signal(sem, where):
        pl.semaphore_signal(sem, inc=1, device_id=where, device_id_type=MESH)

    barrier = pltpu.get_barrier_semaphore()
    tm_peers, along = {}, {}
    for step in (2, 1, 3):
        tm_peers[step] = at(dj=step)
        signal(barrier, tm_peers[step])
    for step in (2, -2, 1, -1):
        along[step] = at(dz=step)
        signal(barrier, along[step])
    sibling = at(flip=True)
    signal(barrier, sibling)
    for step in range(1, n_x):
        signal(barrier, at(dx=step))

    panel_copy = pltpu.make_async_copy(panel_hbm, panel_ref, in_sem.at[0])
    runs_copy = pltpu.make_async_copy(runs_hbm, runs_ref, in_sem.at[1])
    delays_copy = pltpu.make_async_copy(delays_hbm, delays_ref, in_sem.at[2])
    panel_copy.start()
    runs_copy.start()
    delays_copy.start()
    ridge_copy = pltpu.make_async_copy(ridge_hbm, ridge_ref, in_sem.at[3])
    eig_copy = pltpu.make_async_copy(eig_hbm, eig_ref, in_sem.at[4])
    ridge_copy.start()
    eig_copy.start()
    hid_copies = [
        pltpu.make_async_copy(
            hidden_ref.at[:, pl.ds(c * d_chunk, d_chunk)], hid.at[c], hid_sem.at[c]
        )
        for c in range(n_t)
    ]
    for copy in hid_copies:
        copy.start()
    bold_copy = pltpu.make_async_copy(bold_ref, bext.at[pl.ds(0, t_rows)], bold_sem)
    bold_copy.start()

    rows_local = panel_ref.shape[1]
    n_rows = DELAYS * p_local
    block = DELAYS * LANES
    spread = (iota((n_rows, p_local), 0) % p_local == iota((n_rows, p_local), 1)).astype(BF16)
    squeeze = (iota((block, LANES), 0) // DELAYS == iota((block, LANES), 1)).astype(BF16)
    keep = iota((n_rows, rows_local), 1) % DELAYS == iota((n_rows, rows_local), 0) // p_local
    panel_copy.wait()
    tall = dot(spread, panel_ref[...])
    tall = jnp.where(keep, tall, 0.0).astype(BF16)
    for b in range(rows_local // block):
        part = dot(tall[:, b * block:(b + 1) * block], squeeze)
        wbuf[j, :, pl.ds(b * LANES, LANES)] = part.astype(BF16)

    z_peers = {step: along[step] if step in along else at(dz=step) for step in (6, -6, 2, -2)}
    reach = [(dx, dz) for dx in range(n_x) for dz in (-2, -1, 0, 1)]
    reach.sort(key=lambda step: -min(step[0], n_x - step[0]) - abs(step[1]))
    window = [
        at(dx=dx, dz=dz, flip=flip) for dx, dz in reach for flip in (True, False) if dx or dz or flip
    ]

    pl.semaphore_wait(barrier, len(tm_peers) + len(along) + n_x)

    def remote(src, dst, sems, slot, where):
        return pltpu.make_async_remote_copy(
            src_ref=src, dst_ref=dst, send_sem=sems.at[0, slot], recv_sem=sems.at[1, slot],
            device_id=where, device_id_type=MESH,
        )

    w_sends = {s: remote(wbuf.at[j], wbuf.at[j], w_sem, s - 1, tm_peers[s]) for s in (2, 1, 3)}
    for copy in w_sends.values():
        copy.start()
    for where in (*along.values(), sibling):
        signal(near_sem, where)
    tail = HALF * 2 - t_rows - 16
    bext[pl.ds(t_rows + 16, tail), :] = jnp.zeros((tail, LANES), BF16)
    halo = remote(
        bold_ref.at[pl.ds(0, 16)], bext.at[pl.ds(t_rows, 16)], halo_sem, 0, tm_peers[n_t - 1]
    )
    halo.start()

    runs_copy.wait()
    own_runs = runs_ref[:, pl.ds(pl.multiple_of(j * t_rows, LANES), t_rows)]
    next_runs = runs_ref[:, pl.ds(pl.multiple_of(lax.rem(j + 1, n_t) * t_rows, LANES), LANES)]
    runs = jnp.broadcast_to(jnp.concatenate([own_runs, next_runs], 1), (8, ext))
    end = jnp.where(j == n_t - 1, t_rows, ext)
    inside = iota((8, ext), 1) < end
    for m in range(1, MAXD + 1):
        same = (pltpu.roll(runs, m, 1) == runs) & inside
        masks[m - 1] = jnp.where(same, 1.0, 0.0)

    pl.semaphore_wait(near_sem, len(along) + 1)
    signal(far_sem, along[2])
    signal(far_sem, along[-2])
    signal(far_sem, sibling)

    delays_copy.wait()
    shape = (8 * MAXD, n_rows)
    lag = iota(shape, 0) // 8 + 1
    delay_of = iota(shape, 1) // p_local
    right_p = iota(shape, 0) % p_local == iota(shape, 1) % p_local
    wanted = jnp.zeros(shape, jnp.int32)
    for k in range(DELAYS):
        wanted = jnp.where(delay_of == k, delays_ref[k], wanted)
    pick = jnp.where(right_p & (wanted == lag), 1.0, 0.0).astype(BF16)
    pick = jnp.concatenate([pick, pick], 1)

    for copy in hid_copies:
        copy.wait()
    nt = ((1,), (1,))
    g = dot(wbuf[j], hid[j], nt)
    for s in (1, 3, 2):
        w_sends[s].wait_recv()
        source = lax.rem(j + n_t - s, n_t)
        g = g + dot(wbuf[source], hid[source], nt)

    high = g.astype(BF16)
    low = (g - high.astype(F32)).astype(BF16)
    lagged = dot(pick, jnp.concatenate([high, low], 0))
    lagged = jnp.concatenate([lagged, jnp.zeros((8 * MAXD, LANES), F32)], 1)
    gs = jnp.zeros((8, ext), F32)
    for m in range(1, MAXD + 1):
        gs = gs + pltpu.roll(lagged[8 * (m - 1):8 * m], m, 1) * masks[m - 1]

    second = jnp.concatenate([gs[:, HALF:], jnp.zeros((8, 2 * HALF - ext), F32)], 1)
    low_rows = iota((8, HALF), 0) < p_local
    gbuf[...] = jnp.where(low_rows, gs[:, :HALF], second).astype(BF16)
    a_sends = [
        remote(gbuf, abuf.at[f], a_sem, n, where) for n, where in enumerate(z_peers.values())
    ]
    pl.semaphore_wait(far_sem, 3)
    for copy in a_sends:
        copy.start()

    ridge_copy.wait()
    eig_copy.wait()
    n_p = eig_ref.shape[1]
    eig = jnp.broadcast_to(eig_ref[...], (LANES, n_p)).T

    def factor(n, carry):
        level = jnp.full((8, LANES), ridge_ref[n], jnp.int32).astype(F32)
        penalty = jnp.exp2((level - 8.0) * 0.5)
        whole_penalty = jnp.concatenate([penalty] * (n_p // 8), 0)
        scale[n] = 1.0 / (math.sqrt(t_rows * n_t) * (eig + whole_penalty))
        return carry

    lax.fori_loop(0, RIDGES, factor, 0)
    for copy in a_sends:
        copy.wait_recv()
    total = abuf[0].astype(F32)
    for s in range(1, n_f):
        total = total + abuf[s].astype(F32)
    xbuf[group] = total.astype(BF16)

    for where in window:
        pltpu.make_async_remote_copy(
            src_ref=xbuf.at[group], dst_ref=xbuf.at[group],
            send_sem=x_sem.at[0], recv_sem=x_sem.at[1],
            device_id=where, device_id_type=MESH,
        ).start()
    halo.wait_recv()
    bold_copy.wait()
    arrived = xbuf.at[pl.ds(0, n_v - 1)]
    pltpu.make_async_copy(arrived, arrived, x_sem.at[1]).wait()

    sums = xbuf[...].reshape(n_v * 8, HALF)
    wide = jnp.concatenate([bext[pl.ds(h * HALF, HALF), :] for h in range(2)], 1)
    product = dot(sums, wide)
    halves = [product[:, h * LANES:(h + 1) * LANES] for h in range(2)]
    upper = iota((8, LANES), 0) < p_local
    for g2 in range(n_v // 2):
        a, b = slice(16 * g2, 16 * g2 + 8), slice(16 * g2 + 8, 16 * g2 + 16)
        u = jnp.where(upper, halves[0][a], halves[1][b])
        w = jnp.where(upper, halves[0][b], halves[1][a])
        rbuf[j, pl.ds(8 * g2, 8), :] = (u + pltpu.roll(w, 4, 0)).astype(BF16)
    r_sends = [remote(rbuf.at[j], rbuf.at[j], r_sem, s - 1, tm_peers[s]) for s in (2, 1, 3)]
    for copy in r_sends:
        copy.start()
    for copy in r_sends:
        copy.wait_recv()
    rotated = rbuf[0].astype(F32)
    for s in range(1, n_t):
        rotated = rotated + rbuf[s].astype(F32)
    for n in range(RIDGES):
        out_ref[n] = (rotated * scale[n]).astype(BF16)

    for copy in [*w_sends.values(), *a_sends, *r_sends, halo]:
        copy.wait_send()
    pltpu.make_async_copy(arrived, arrived, x_sem.at[0]).wait()


def shards(hidden, bold, panel, eigvals, ridge_grid, delays, runs):
    n_v, n_f, n_t = (lax.axis_size(axis) for axis in ("voxel", "feature", "tm"))
    t_rows, d_local = hidden.shape
    v_cols = bold.shape[1]
    p_local = panel.shape[1]
    n_p = n_v * p_local
    ext = t_rows + LANES
    d_chunk = d_local // n_t
    hbm = pl.BlockSpec(memory_space=pl.ANY)
    dma = pltpu.SemaphoreType.DMA
    return pl.pallas_call(
        functools.partial(kernel, (n_v, n_f, n_t, t_rows, d_local, p_local)),
        out_shape=pltpu.VMEM((RIDGES, n_p, v_cols), BF16),
        in_specs=[hbm] * 7,
        out_specs=pl.BlockSpec(memory_space=pltpu.VMEM),
        scratch_shapes=[
            pltpu.SMEM((DELAYS,), jnp.int32),
            pltpu.SMEM((RIDGES,), jnp.int32),
            pltpu.VMEM((p_local, panel.shape[0]), BF16),
            pltpu.VMEM((1, runs.shape[0]), jnp.int32),
            pltpu.VMEM((1, n_p), F32),
            pltpu.VMEM((RIDGES, n_p, v_cols), F32),
            pltpu.VMEM((n_t, t_rows, d_chunk), BF16),
            pltpu.VMEM((2 * HALF, v_cols), BF16),
            pltpu.VMEM((n_t, DELAYS * p_local, d_chunk), BF16),
            pltpu.VMEM((8, HALF), BF16),
            pltpu.VMEM((n_f, 8, HALF), BF16),
            pltpu.VMEM((n_v, 8, HALF), BF16),
            pltpu.VMEM((n_t, n_p, v_cols), BF16),
            pltpu.VMEM((MAXD, 8, ext), F32),
            dma((5,)),
            dma((n_t,)),
            dma,
            dma((2, 1)),
            dma((2, n_t - 1)),
            dma((2, n_f)),
            dma((2,)),
            dma((2, n_t - 1)),
            pltpu.SemaphoreType.REGULAR,
            pltpu.SemaphoreType.REGULAR,
        ],
        compiler_params=pltpu.CompilerParams(collective_id=0, has_side_effects=True),
        name="sweep",
    )(delays, ridge_grid, hidden, bold, panel.T, runs[None], eigvals[None])


def solution(mesh):
    return jax.shard_map(
        shards,
        mesh=mesh,
        in_specs=(
            P("tm", "feature"),
            P("tm", "voxel"),
            P(("feature", "tm"), "voxel"),
            P(),
            P(),
            P(),
            P(),
        ),
        out_specs=P(None, None, "voxel"),
        check_vma=False,
    )
```
